32 devices in a mesh: wide: 8 (over z, core), narrow: 4 (over y, x).
Axes of the slice: x: 2, y: 2, z: 4, core: 2. Of those that a mesh axis runs over, the one named last changes fastest.
Arguments:
- inputs: bfloat16 [4096, 1024], P(('wide', 'narrow')), may hold values from -6 to 6
- cotangent: bfloat16 [4096, 1024], P(('wide', 'narrow')), may hold values from -6 to 6
- seq_len: int32 [32], replicated, may hold values from 16 to 128, as said below
- shallow_routes: int32 [4096, 1], replicated, may hold values from 0 to 7; in each aligned block of 128 rows (0 to 127, 128 to 255, ...) at most 24 rows name the same one
- deep_routes: int32 [4096, 1], replicated, may hold values from 0 to 15; in each aligned block of 128 rows (0 to 127, 128 to 255, ...) at most 12 rows name the same one
- shallow_norm_first: bfloat16 [1024], P('wide'), may hold values from 0.5 to 1.5
- shallow_attention_in: bfloat16 [1024, 3072], P('wide'), may hold values from -0.1875 to 0.1875
- shallow_attention_out: bfloat16 [1024, 1024], P('wide'), may hold values from -1 to 1
- shallow_norm_second: bfloat16 [1024], P('wide'), may hold values from 0.5 to 1.5
- shallow_dense_up: bfloat16 [1024, 4096], P(None, 'wide'), may hold values from -0.1875 to 0.1875
- shallow_dense_down: bfloat16 [4096, 1024], P('wide'), may hold values from -0.1875 to 0.1875
- shallow_mixer: bfloat16 [1024, 2], P('wide'), may hold values from -0.09375 to 0.09375
- shallow_expert_up: bfloat16 [32, 1024, 1024], P(('wide', 'narrow')), may hold values from -0.1875 to 0.1875
- shallow_expert_down: bfloat16 [32, 1024, 1024], P(('wide', 'narrow')), may hold values from -0.1875 to 0.1875
- deep_norm_first: bfloat16 [1024], P('wide'), may hold values from 0.5 to 1.5
- deep_attention_in: bfloat16 [1024, 3072], P('wide'), may hold values from -0.1875 to 0.1875
- deep_attention_out: bfloat16 [1024, 1024], P('wide'), may hold values from -1 to 1
- deep_norm_second: bfloat16 [1024], P('wide'), may hold values from 0.5 to 1.5
- deep_dense_up: bfloat16 [1024, 4096], P(None, 'wide'), may hold values from -0.1875 to 0.1875
- deep_dense_down: bfloat16 [4096, 1024], P('wide'), may hold values from -0.1875 to 0.1875
- deep_mixer: bfloat16 [1024, 2], P('wide'), may hold values from -0.09375 to 0.09375
- deep_expert_up: bfloat16 [32, 1024, 2048], P(('wide', 'narrow')), may hold values from -0.1875 to 0.1875
- deep_expert_down: bfloat16 [32, 2048, 1024], P(('wide', 'narrow')), may hold values from -0.1875 to 0.1875
Outputs:
- result: bfloat16 [4096, 1024], P(('wide', 'narrow'))
- grad_inputs: float32 [4096, 1024], P(('wide', 'narrow'))
- grad_shallow_norm_first: float32 [1024], P('wide')
- grad_shallow_attention_in: float32 [1024, 3072], P('wide')
- grad_shallow_attention_out: float32 [1024, 1024], P('wide')
- grad_shallow_norm_second: float32 [1024], P('wide')
- grad_shallow_dense_up: float32 [1024, 4096], P(None, 'wide')
- grad_shallow_dense_down: float32 [4096, 1024], P('wide')
- grad_shallow_mixer: float32 [1024, 2], P('wide')
- grad_shallow_expert_up: float32 [32, 1024, 1024], P(('wide', 'narrow'))
- grad_shallow_expert_down: float32 [32, 1024, 1024], P(('wide', 'narrow'))
- grad_deep_norm_first: float32 [1024], P('wide')
- grad_deep_attention_in: float32 [1024, 3072], P('wide')
- grad_deep_attention_out: float32 [1024, 1024], P('wide')
- grad_deep_norm_second: float32 [1024], P('wide')
- grad_deep_dense_up: float32 [1024, 4096], P(None, 'wide')
- grad_deep_dense_down: float32 [4096, 1024], P('wide')
- grad_deep_mixer: float32 [1024, 2], P('wide')
- grad_deep_expert_up: float32 [32, 1024, 2048], P(('wide', 'narrow'))
- grad_deep_expert_down: float32 [32, 2048, 1024], P(('wide', 'narrow'))
The draws below stay inside these ranges and needn't reach their ends.
Inputs may be any that keep to these rules, and one draw needn't show every extreme that they name: Sequence s holds real tokens in its first seq_len[s] slots; some sequence fills all 128. `shallow_routes`: among the 128 rows of one sequence (aligned blocks), no expert is named more than 24 times, and in some sequence one is named exactly that often. `deep_routes`: among the 128 rows of one sequence (aligned blocks), no expert is named more than 12 times, and in some sequence one is named exactly that often.
All inputs are finite; a program needn't handle non-finite values.
Results may differ from the reference program's by a relative error of at most 0.03.
Values may be sent and summed in bfloat16 or wider, within the bound.
No kernel may reach another device: no remote copies, remote signals or barrier semaphores. Data moves between devices by JAX's collectives and lax.ppermute only.
A program may use at most 320 MiB of HBM per device.

```python
import math
import jax
import jax.numpy as jnp
import numpy as np
from jax import lax

D = 1024
HEADS = 16
HEAD_DIM = 64
FF = 4096
SEQ = 128
GROUP_SHALLOW = 4
GROUP_DEEP = 2
SEQS = 32
TOKENS = 4096
EXP_SHALLOW = 8
EXP_DEEP = 16
CAP_SHALLOW = 24
CAP_DEEP = 12


def draw_seq_len(key, part):
    key_one, key_two = jax.random.split(key)
    lengths = jax.random.randint(key_one, (SEQS,), SEQ // 8, SEQ + 1, dtype=jnp.int32)
    chosen = jax.random.randint(key_two, (), 0, SEQS, dtype=jnp.int32)
    return jnp.where(jnp.arange(SEQS, dtype=jnp.int32) == chosen, SEQ, lengths).astype(jnp.int32)


def block_levels(own_key, extent, cuts, low, top_value):
    def one(axis_at, parts):
        heights = jax.random.uniform(jax.random.fold_in(jax.random.fold_in(own_key, 6), axis_at), (parts,), jnp.float32, low / len(cuts), top_value / len(cuts))
        return jnp.repeat(jnp.exp(heights), extent[axis_at] // parts).reshape((-1,) + (1,) * (len(extent) - axis_at - 1))

    level = one(*cuts[0])
    for cut in cuts[1:]:
        level = level * one(*cut)
    return level


def shared_out(rng, own, number, rows, number_of, top, bound, slope):
    sequence = jax.random.permutation(rng, number_of)
    crowded, usual = shares(number_of, rows * top, bound, slope, True), shares(number_of, rows * top, bound, slope, False)
    places = jnp.arange(number_of)

    def named(sizes, turn):
        used = int((sizes > 0).sum())
        fixed = max(1, used // 4)
        passed = fixed + (places - fixed + turn * (used - fixed)) % max(1, number_of - fixed)
        return jnp.zeros((number_of,), jnp.int32).at[sequence[jnp.where(places < fixed, places, passed)]].set(jnp.asarray(sizes, jnp.int32))

    sizes = jnp.where(number % 4 == 0, named(crowded, number // 4), named(usual, number - number // 4 - 1))
    mixed = jax.random.permutation(jax.random.fold_in(own, 3), number_of)
    donor, receiver = mixed[0:number_of // 2 * 2:2], mixed[1:number_of // 2 * 2:2]
    room = jnp.minimum(sizes[donor] - 1, bound - sizes[receiver]) // 2
    room = jnp.where((donor == sequence[0]) | (receiver == sequence[0]) | (sizes[receiver] == 0), 0, jnp.maximum(room, 0))
    passed = jax.random.randint(jax.random.fold_in(own, 4), (number_of // 2,), 0, 1 << 20) % (room + 1)
    sizes = sizes.at[donor].add(-passed).at[receiver].add(passed)
    members = jnp.searchsorted(jnp.cumsum(sizes), jnp.arange(rows * top), side="right").astype(jnp.int32)
    grid = members.reshape(top, rows).T
    grid = grid[jax.random.permutation(jax.random.fold_in(own, 1), rows)]
    turn = jax.random.randint(jax.random.fold_in(own, 2), (rows, 1), 0, top)
    return jnp.take_along_axis(grid, (jnp.arange(top)[None, :] + turn) % top, axis=1)


def shares(amount, total, limit, lean, full):
    weights = [(1 << 20) // math.isqrt(grade ** lean) + 1 for grade in range(1, amount + 1)]
    largest = limit if full else min(limit, max(-(-total // amount), total * weights[0] // sum(weights)))
    least = 1 if total - largest >= amount - 1 else 0
    holding, spare = [largest] + [least] * (amount - 1), total - largest - least * (amount - 1)
    while spare > 0:
        free = [i for i in range(1, amount) if holding[i] < largest] or [i for i in range(1, amount) if holding[i] < limit]
        pool, remaining = sum([weights[i] for i in free]), spare
        for i in free:
            more = min(limit - holding[i], max(1, remaining * weights[i] // pool), spare)
            holding[i] = holding[i] + more
            spare = spare - more
    return np.array(holding)


def gaussian(rng, extent, scale, limit, shards=(), kind=jnp.bfloat16):
    drawn = scale * jax.random.normal(rng, extent, jnp.float32)
    if shards:
        drawn = drawn * block_levels(rng, extent, shards, -0.22, 0.18)
    return jnp.clip(drawn, -limit, limit).astype(kind)


def setup_inputs(seed: int = 0) -> dict:
    key_list = jax.random.split(jax.random.key(seed), 24)
    inputs = gaussian(key_list[0], (TOKENS, D), 1.0, 6.0, ((0, 32),))
    cotangent = gaussian(key_list[1], (TOKENS, D), 1.0, 6.0, ((0, 32),))
    seq_len = draw_seq_len(jax.random.fold_in(key_list[23], 71), 0)
    shallow_routes_keys = jax.random.split(jax.random.fold_in(key_list[3], 1), TOKENS // SEQ)
    shallow_routes_turns = jax.random.permutation(jax.random.fold_in(key_list[3], 3), TOKENS // SEQ)
    shallow_routes = jax.vmap(lambda own, number: shared_out(jax.random.fold_in(key_list[3], 2), own, number, SEQ, EXP_SHALLOW, 1, CAP_SHALLOW, 1))(shallow_routes_keys, shallow_routes_turns).reshape((TOKENS, 1))
    deep_routes_keys = jax.random.split(jax.random.fold_in(key_list[4], 1), TOKENS // SEQ)
    deep_routes_turns = jax.random.permutation(jax.random.fold_in(key_list[4], 3), TOKENS // SEQ)
    deep_routes = jax.vmap(lambda own, number: shared_out(jax.random.fold_in(key_list[4], 2), own, number, SEQ, EXP_DEEP, 1, CAP_DEEP, 1))(deep_routes_keys, deep_routes_turns).reshape((TOKENS, 1))
    shallow_norm_first = jnp.clip(1.0 + 0.1 * jax.random.normal(key_list[5], (D,), jnp.float32), 0.5, 1.5).astype(jnp.bfloat16)
    shallow_attention_in = gaussian(key_list[6], (D, 3 * D), D ** -0.5, 0.1875, ((0, 8),))
    shallow_attention_out = gaussian(key_list[7], (D, D), (D // 32) ** -0.5, 1.0, ((0, 8),))
    shallow_norm_second = jnp.clip(1.0 + 0.1 * jax.random.normal(key_list[8], (D,), jnp.float32), 0.5, 1.5).astype(jnp.bfloat16)
    shallow_dense_up = gaussian(key_list[9], (D, FF), D ** -0.5, 0.1875, ((1, 8),))
    shallow_dense_down = gaussian(key_list[10], (FF, D), (FF // 4) ** -0.5, 0.1875, ((0, 8),))
    shallow_mixer = gaussian(key_list[11], (D, 2), (4 * D) ** -0.5, 0.09375, ((0, 8),))
    shallow_expert_up = gaussian(key_list[12], (EXP_SHALLOW * GROUP_SHALLOW, D, FF // GROUP_SHALLOW), D ** -0.5, 0.1875, ((0, 32),))
    shallow_expert_down = gaussian(key_list[13], (EXP_SHALLOW * GROUP_SHALLOW, FF // GROUP_SHALLOW, D), (FF // 4) ** -0.5, 0.1875, ((0, 32),))
    deep_norm_first = jnp.clip(1.0 + 0.1 * jax.random.normal(key_list[14], (D,), jnp.float32), 0.5, 1.5).astype(jnp.bfloat16)
    deep_attention_in = gaussian(key_list[15], (D, 3 * D), D ** -0.5, 0.1875, ((0, 8),))
    deep_attention_out = gaussian(key_list[16], (D, D), (D // 32) ** -0.5, 1.0, ((0, 8),))
    deep_norm_second = jnp.clip(1.0 + 0.1 * jax.random.normal(key_list[17], (D,), jnp.float32), 0.5, 1.5).astype(jnp.bfloat16)
    deep_dense_up = gaussian(key_list[18], (D, FF), D ** -0.5, 0.1875, ((1, 8),))
    deep_dense_down = gaussian(key_list[19], (FF, D), (FF // 4) ** -0.5, 0.1875, ((0, 8),))
    deep_mixer = gaussian(key_list[20], (D, 2), (4 * D) ** -0.5, 0.09375, ((0, 8),))
    deep_expert_up = gaussian(key_list[21], (EXP_DEEP * GROUP_DEEP, D, FF // GROUP_DEEP), D ** -0.5, 0.1875, ((0, 32),))
    deep_expert_down = gaussian(key_list[22], (EXP_DEEP * GROUP_DEEP, FF // GROUP_DEEP, D), (FF // 4) ** -0.5, 0.1875, ((0, 32),))
    return {"inputs": inputs, "cotangent": cotangent, "seq_len": seq_len, "shallow_routes": shallow_routes, "deep_routes": deep_routes, "shallow_norm_first": shallow_norm_first, "shallow_attention_in": shallow_attention_in, "shallow_attention_out": shallow_attention_out, "shallow_norm_second": shallow_norm_second, "shallow_dense_up": shallow_dense_up, "shallow_dense_down": shallow_dense_down, "shallow_mixer": shallow_mixer, "shallow_expert_up": shallow_expert_up, "shallow_expert_down": shallow_expert_down, "deep_norm_first": deep_norm_first, "deep_attention_in": deep_attention_in, "deep_attention_out": deep_attention_out, "deep_norm_second": deep_norm_second, "deep_dense_up": deep_dense_up, "deep_dense_down": deep_dense_down, "deep_mixer": deep_mixer, "deep_expert_up": deep_expert_up, "deep_expert_down": deep_expert_down}


@jax.custom_vjp
def low(v):
    return lax.optimization_barrier(v.astype(jnp.bfloat16)).astype(jnp.float32)

@jax.custom_vjp
def low_back(v):
    return v

def low_keep(v):
    return (low(v), None)

def low_pass(kept, grad):
    return (grad,)

def back_keep(v):
    return (v, None)

def back_low(kept, grad):
    return (low(grad),)
low.defvjp(low_keep, low_pass)
low_back.defvjp(back_keep, back_low)
precise = lax.Precision.HIGHEST

def layer_norm(source, gain_vector):
    centre = source - lax.optimization_barrier(jnp.mean(source, axis=-1, keepdims=True))
    spread = lax.optimization_barrier(jnp.mean(centre * centre, axis=-1, keepdims=True))
    return centre * lax.rsqrt(spread + 1e-05) * gain_vector

def attend_one(pair):
    packed_seq, length = pair
    queries = packed_seq[:, :D].reshape(SEQ, HEADS, HEAD_DIM)
    key_rows = packed_seq[:, D:2 * D].reshape(SEQ, HEADS, HEAD_DIM)
    values = packed_seq[:, 2 * D:].reshape(SEQ, HEADS, HEAD_DIM)
    scores = low_back(jnp.einsum('qhd,khd->hqk', queries, key_rows, precision=precise) * HEAD_DIM ** (-0.5))
    places = jnp.arange(SEQ, dtype=jnp.int32)
    allowed = (places[None, :] <= places[:, None]) & (places[None, :] < length)
    scores = jnp.where(allowed[None], scores, -1e+30)
    softened = jax.nn.softmax(scores, axis=-1)
    return jnp.einsum('hqk,khd->qhd', low(softened), values, precision=precise).reshape(SEQ, D)

def expert_layer(expert_in, routes, expert_up, expert_down, group_size, capacity):
    experts = expert_up.shape[0] // group_size
    labels = routes[:, 0].astype(jnp.int32)
    by_seq = labels.reshape(SEQS, SEQ)
    one_hot = (by_seq[:, :, None] == jnp.arange(experts, dtype=jnp.int32)[None, None, :]).astype(jnp.int32)
    ranking = lax.optimization_barrier(jnp.sum(jnp.cumsum(one_hot, axis=1) * one_hot, axis=-1)) - 1
    row_index = (jnp.arange(SEQS, dtype=jnp.int32)[:, None] * capacity + ranking).reshape(-1).astype(jnp.int32)
    buffer = jnp.zeros((experts, SEQS * capacity, D), jnp.float32).at[labels, row_index].set(expert_in)
    weights_in = expert_up.reshape(experts, group_size, D, FF // group_size).transpose(0, 2, 1, 3).reshape(experts, D, FF)
    weights_out = expert_down.reshape(experts, FF, D)

    def one_expert(triple):
        block_rows, w_in, w_out = triple
        hidden = low_back(jnp.dot(block_rows, w_in, precision=precise))
        return jnp.dot(low(jax.nn.gelu(hidden)), w_out, precision=precise)
    outcome = lax.map(jax.checkpoint(one_expert), (buffer, weights_in, weights_out))
    outcome = low_back(low(outcome))
    return outcome[labels, row_index]

def block_forward(inputs, norm_first, attention_in, attention_out, norm_second, dense_up, dense_down, mixer, expert_up, expert_down, routes, seq_len, group_size, capacity):
    normed = low(layer_norm(inputs, norm_first))
    packed = low_back(low(jnp.dot(normed, attention_in, precision=precise)))
    context = lax.map(jax.checkpoint(attend_one), (packed.reshape(SEQS, SEQ, 3 * D), seq_len))
    context = low(low_back(context.reshape(TOKENS, D)))
    middle = inputs + low_back(jnp.dot(context, attention_out, precision=precise))
    second = low(layer_norm(middle, norm_second))
    pre_dense = low_back(jnp.dot(second, dense_up, precision=precise))
    dense_result = low_back(jnp.dot(low(jax.nn.gelu(pre_dense)), dense_down, precision=precise))
    mixing = jax.nn.softmax(low_back(jnp.dot(second, mixer, precision=precise)), axis=-1)
    expert_result = expert_layer(low_back(second), routes, expert_up, expert_down, group_size, capacity)
    return middle + mixing[:, :1] * dense_result + mixing[:, 1:] * expert_result

def reference(inputs, cotangent, seq_len, shallow_routes, deep_routes, shallow_norm_first, shallow_attention_in, shallow_attention_out, shallow_norm_second, shallow_dense_up, shallow_dense_down, shallow_mixer, shallow_expert_up, shallow_expert_down, deep_norm_first, deep_attention_in, deep_attention_out, deep_norm_second, deep_dense_up, deep_dense_down, deep_mixer, deep_expert_up, deep_expert_down):
    floats = (inputs, shallow_norm_first, shallow_attention_in, shallow_attention_out, shallow_norm_second, shallow_dense_up, shallow_dense_down, shallow_mixer, shallow_expert_up, shallow_expert_down, deep_norm_first, deep_attention_in, deep_attention_out, deep_norm_second, deep_dense_up, deep_dense_down, deep_mixer, deep_expert_up, deep_expert_down)
    floats = tuple((argument.astype(jnp.float32) for argument in floats))

    def both_blocks(source, *parameters):
        middle = block_forward(source, *parameters[:9], shallow_routes, seq_len, GROUP_SHALLOW, CAP_SHALLOW)
        return block_forward(middle, *parameters[9:], deep_routes, seq_len, GROUP_DEEP, CAP_DEEP)
    outcome, pullback = jax.vjp(both_blocks, *floats)
    gradients = pullback(cotangent.astype(jnp.float32))
    return (outcome.astype(jnp.bfloat16), gradients[0], gradients[1], gradients[2], gradients[3], gradients[4], gradients[5], gradients[6], gradients[7], gradients[8], gradients[9], gradients[10], gradients[11], gradients[12], gradients[13], gradients[14], gradients[15], gradients[16], gradients[17], gradients[18])
```

```python
import jax
import jax.numpy as jnp
from jax import lax
from jax.experimental import pallas as pl
from jax.experimental.pallas import tpu as pltpu
from jax.sharding import PartitionSpec as P

HEAD_DIM = 64
SLICES_SHALLOW = 4
SLICES_DEEP = 2
F32 = jnp.float32
LOW = jnp.bfloat16
VMEM_LIMIT = 60 * 1024 * 1024


def low(value):
    return value.astype(LOW)


def swap(array, axis, distance):
    return lax.ppermute(array, axis, [(i, i ^ distance) for i in range(lax.axis_size(axis))])


def product(left, right, left_dim, right_dim):
    return lax.dot_general(
        left, right, (((left_dim,), (right_dim,)), ((), ())), preferred_element_type=F32
    )


def vmem():
    return pl.BlockSpec(memory_space=pltpu.VMEM)


def smem():
    return pl.BlockSpec(memory_space=pltpu.SMEM)


def call(kernel, outs, scalars, arrays, scratch=(), flops=0):
    moved = sum(a.size * a.dtype.itemsize for a in list(arrays) + list(outs))
    return pl.pallas_call(
        kernel,
        out_shape=tuple(outs),
        in_specs=[smem()] * len(scalars) + [vmem()] * len(arrays),
        out_specs=tuple(vmem() for _ in outs),
        scratch_shapes=list(scratch),
        compiler_params=pltpu.CompilerParams(vmem_limit_bytes=VMEM_LIMIT),
        cost_estimate=pl.CostEstimate(flops=flops, bytes_accessed=moved, transcendentals=0),
    )(*scalars, *arrays)


def shape(dims, kind):
    return jax.ShapeDtypeStruct(dims, kind)


def pack_rows(pieces, base):
    count, (rows, columns) = len(pieces), pieces[0].shape

    def kernel(base_ref, *refs):
        for k in range(count):
            start = pl.multiple_of((base_ref[0] ^ k) * rows, rows)
            refs[count][pl.ds(start, rows), :] = refs[k][...]

    outs = [shape((count * rows, columns), pieces[0].dtype)]
    return call(kernel, outs, [base], pieces)[0]


def join_rows(pieces):
    if len(pieces) == 1:
        return pieces[0]
    count, (rows, columns) = len(pieces), pieces[0].shape

    def kernel(*refs):
        for k in range(count):
            refs[count][k * rows : (k + 1) * rows, :] = refs[k][...]

    return call(kernel, [shape((count * rows, columns), pieces[0].dtype)], [], pieces)[0]


def pack_columns(pieces, base):
    count, (rows, columns) = len(pieces), pieces[0].shape

    def kernel(base_ref, *refs):
        for k in range(count):
            start = pl.multiple_of((base_ref[0] ^ k) * columns, columns)
            refs[count][:, pl.ds(start, columns)] = refs[k][...]

    return call(kernel, [shape((rows, count * columns), pieces[0].dtype)], [base], pieces)[0]


def split_columns(whole, count, base):
    rows, columns = whole.shape[0], whole.shape[1] // count

    def kernel(base_ref, whole_ref, *outs):
        for k in range(count):
            start = pl.multiple_of((base_ref[0] ^ k) * columns, columns)
            outs[k][...] = low(whole_ref[:, pl.ds(start, columns)])

    return call(kernel, [shape((rows, columns), LOW)] * count, [base], [whole])


def reversed_order(count):
    bits = count.bit_length() - 1
    return [sum((i >> b & 1) << (bits - 1 - b) for b in range(bits)) for i in range(count)]


def split_halves(whole, count, base):
    rows, columns = whole.shape[0] // count, whole.shape[1]
    order = reversed_order(count)

    def kernel(base_ref, whole_ref, keep_ref, send_ref):
        for i, k in enumerate(order):
            start = pl.multiple_of((base_ref[0] ^ k) * rows, rows)
            block = low(whole_ref[pl.ds(start, rows), :])
            out, at = (keep_ref, i) if i < count // 2 else (send_ref, i - count // 2)
            out[at * rows : (at + 1) * rows, :] = block

    return call(kernel, [shape((rows * count // 2, columns), LOW)] * 2, [base], [whole])


def scatter_halves(keep, send):
    distance = 1
    wide = lax.axis_size("wide")
    while True:
        total = keep.astype(F32) + swap(send, "wide", distance).astype(F32)
        distance *= 2
        if distance == wide:
            return total
        half = total.shape[0] // 2
        keep, send = total[:half], low(total[half:])


def narrow_sum(value, first):
    narrow = lax.axis_size("narrow")
    bits = narrow.bit_length() - 1
    for b in range(bits):
        value = value + swap(low(value), "narrow", 1 << (b + first) % bits).astype(F32)
    return value


def everywhere_sum(value):
    for axis in ("narrow", "wide"):
        distance = 1
        while distance < lax.axis_size(axis):
            value = value + swap(value, axis, distance)
            distance *= 2
    return value


def layer_norm(source, gain):
    centre = source - jnp.mean(source, axis=-1, keepdims=True)
    inverse = lax.rsqrt(jnp.mean(centre * centre, axis=-1, keepdims=True) + 1e-05)
    scaled = centre * inverse
    return scaled * gain, scaled, inverse


def norm_back(upstream, scaled, inverse, gain):
    grad_scaled = upstream * gain
    mean_first = jnp.mean(grad_scaled, axis=-1, keepdims=True)
    mean_second = jnp.mean(grad_scaled * scaled, axis=-1, keepdims=True)
    return (
        inverse * (grad_scaled - mean_first - scaled * mean_second),
        jnp.sum(upstream * scaled, axis=0),
    )


def activate(source):
    return jax.nn.gelu(source)


def activation_back(source, upstream):
    return jax.vjp(activate, source)[1](upstream)[0]


def softened_scores(queries, keys, allowed):
    scores = product(queries, keys, 1, 1) * HEAD_DIM ** (-0.5)
    scores = jnp.where(allowed, scores, -1e30)
    raised = jnp.exp(scores - jnp.max(scores, axis=-1, keepdims=True))
    return raised / jnp.sum(raised, axis=-1, keepdims=True)


def allowed_of(length, slots):
    rows_at = lax.broadcasted_iota(jnp.int32, (slots, slots), 0)
    cols_at = lax.broadcasted_iota(jnp.int32, (slots, slots), 1)
    return (cols_at <= rows_at) & (cols_at < length)


def head_parts(packed, head, columns):
    return [
        packed[:, part * columns + head * HEAD_DIM : part * columns + (head + 1) * HEAD_DIM]
        for part in range(3)
    ]


def attention(pieces, weight, lengths):
    count, (slots, features) = len(pieces), pieces[0].shape
    columns = weight.shape[1] // 3

    def kernel(lengths_ref, *refs):
        ins, weight_ref, packed_ref, outs = (
            refs[:count], refs[count], refs[count + 1], refs[count + 2 :],
        )
        for j in range(count):
            packed = low(product(ins[j][...], weight_ref[...], 1, 0))
            packed_ref[j] = packed
            allowed = allowed_of(lengths_ref[j], slots)
            found = []
            for head in range(columns // HEAD_DIM):
                queries, keys, values = head_parts(packed, head, columns)
                softened = softened_scores(queries, keys, allowed)
                found.append(product(low(softened), values, 1, 0))
            outs[j][...] = low(jnp.concatenate(found, axis=1))

    outs = [shape((count, slots, 3 * columns), LOW)] + [shape((slots, columns), LOW)] * count
    flops = 2 * count * slots * features * 3 * columns
    packed, *contexts = call(kernel, outs, [lengths], list(pieces) + [weight], flops=flops)
    return packed, contexts


def attention_back(pieces, weight, packed, grads, lengths):
    count, (slots, features) = len(pieces), pieces[0].shape
    columns = weight.shape[1] // 3
    scaling = HEAD_DIM ** (-0.5)

    def kernel(lengths_ref, *refs):
        ins, weight_ref, packed_ref = refs[:count], refs[count], refs[count + 1]
        grad_refs = refs[count + 2 : 2 * count + 2]
        total_ref, outs = refs[2 * count + 2], refs[2 * count + 3 :]
        for j in range(count):
            allowed = allowed_of(lengths_ref[j], slots)
            whole = packed_ref[j]
            grad_whole = grad_refs[j][...]
            found = [[], [], []]
            for head in range(columns // HEAD_DIM):
                queries, keys, values = head_parts(whole, head, columns)
                grad_head = grad_whole[:, head * HEAD_DIM : (head + 1) * HEAD_DIM]
                softened = softened_scores(queries, keys, allowed)
                grad_soft = product(grad_head, values, 1, 1)
                inner = jnp.sum(softened * grad_soft, axis=-1, keepdims=True)
                grad_scores = low(softened * (grad_soft - inner))
                found[0].append(scaling * product(grad_scores, keys, 1, 0))
                found[1].append(scaling * product(grad_scores, queries, 0, 0))
                found[2].append(product(low(softened), grad_head, 0, 0))
            grad_packed = low(jnp.concatenate(found[0] + found[1] + found[2], axis=1))
            added = product(ins[j][...], grad_packed, 0, 0)
            if j == 0:
                total_ref[...] = added
            else:
                total_ref[...] += added
            outs[j][...] = low(product(grad_packed, weight_ref[...], 1, 1))

    outs = [shape((features, 3 * columns), F32)] + [shape((slots, features), LOW)] * count
    flops = 4 * count * slots * features * 3 * columns
    arrays = list(pieces) + [weight, packed] + list(grads)
    total, *parts = call(kernel, outs, [lengths], arrays, flops=flops)
    return total, parts


def chunks_of(wide):
    return [list(range(0, wide, 2))]


def wide_pieces(own):
    across = [own]
    for apart in range(2, lax.axis_size("wide"), 2):
        across.append(swap(own, "wide", apart))
    return across, [swap(piece, "wide", 1) for piece in across]


def wide_join(across, beside, chunk):
    return join_rows([across[a // 2] for a in chunk] + [beside[a // 2] for a in chunk])


def chunk_order(chunk):
    return list(chunk) + [a + 1 for a in chunk]


def wide_sums(chunks, merged, slots):
    total = None
    for chunk, value in zip(chunks, merged):
        half = value.shape[0] // 2
        pair = value[:half] + swap(low(value[half:]), "wide", 1).astype(F32)
        for i, apart in enumerate(chunk):
            part = pair[i * slots : (i + 1) * slots]
            if apart:
                part = swap(low(part), "wide", apart).astype(F32)
            total = part if total is None else total + part
    return total


def place(labels, experts, capacity):
    places = jnp.arange(capacity, dtype=jnp.int32)
    selects = []
    for expert in experts:
        chosen = labels == expert
        rank = jnp.where(chosen, jnp.cumsum(chosen.astype(jnp.int32), axis=1) - 1, -1)
        selects.append(low(rank[:, None, :] == places[None, :, None]))
    return selects


def to_experts(selects, rows, slices):
    features = rows.shape[-1]
    blocks, capacity, slots = selects[0].shape
    rows = rows.reshape(blocks, slots, features)
    sent = [
        low(
            lax.dot_general(s, rows, (((2,), (1,)), ((0,), (0,))), preferred_element_type=F32)
        ).reshape(blocks * capacity, features)
        for s in selects
    ]
    narrow = lax.axis_size("narrow")
    return join_rows(
        [sent[j // slices] if j == 0 else swap(sent[j // slices], "narrow", j) for j in range(narrow)]
    )


def from_experts(selects, outcome, slices):
    blocks, capacity, slots = selects[0].shape
    narrow = lax.axis_size("narrow")
    features = outcome.shape[-1]
    parts = outcome.reshape(narrow, blocks * capacity, features)
    spread = None
    for r, select in enumerate(selects):
        total = None
        for j in range(r * slices, (r + 1) * slices):
            part = parts[j] if j == 0 else swap(low(parts[j]), "narrow", j).astype(F32)
            total = part if total is None else total + part
        rows = low(total).reshape(blocks, capacity, features)
        part = lax.dot_general(
            select, rows, (((1,), (1,)), ((0,), (0,))), preferred_element_type=F32
        )
        spread = part if spread is None else spread + part
    return spread.reshape(-1, features)


def layer_forward(source, weights, selects, lengths, at_narrow, slices):
    norm_first, attention_in, attention_out, norm_second, mixer, up, down, expert_up, expert_down = weights
    slots, features = source.shape
    wide, narrow = lax.axis_size("wide"), lax.axis_size("narrow")
    normed, scaled_one, inverse_one = layer_norm(source, norm_first)
    normed_low = low(normed)
    pieces = [normed_low] + [swap(normed_low, "narrow", j) for j in range(1, narrow)]
    packed, contexts = attention(pieces, attention_in, lengths)
    context = pack_columns(
        [contexts[0]] + [swap(contexts[j], "narrow", j) for j in range(1, narrow)], at_narrow
    )
    middle = source + jnp.dot(context, attention_out, preferred_element_type=F32)
    second, scaled_two, inverse_two = layer_norm(middle, norm_second)
    across, beside = wide_pieces(low(second))
    chunks = chunks_of(wide)
    merged, kept_chunks = [], []
    for chunk, select in zip(chunks, selects):
        rows = wide_join(across, beside, chunk)
        mixing = jax.nn.softmax(jnp.dot(rows, mixer, preferred_element_type=F32), axis=-1)
        expert_rows = to_experts(select, rows, slices)
        expert_pre = jnp.dot(expert_rows, expert_up, preferred_element_type=F32)
        expert_act = low(activate(expert_pre))
        outcome = jnp.dot(expert_act, expert_down, preferred_element_type=F32)
        pre = jnp.dot(rows, up, preferred_element_type=F32)
        act = low(activate(pre))
        dense = jnp.dot(act, down, preferred_element_type=F32)
        spread = from_experts(select, outcome, slices)
        merged.append(mixing[:, :1] * dense + mixing[:, 1:] * spread)
        kept_chunks.append((rows, mixing, expert_rows, expert_pre, expert_act, pre, act))
    output = middle + wide_sums(chunks, merged, slots)
    kept = (scaled_one, inverse_one, pieces, packed, context, scaled_two, inverse_two, kept_chunks)
    return output, kept


def layer_backward(upstream, kept, weights, selects, lengths, at_narrow, at_wide, slices):
    norm_first, attention_in, attention_out, norm_second, mixer, up, down, expert_up, expert_down = weights
    scaled_one, inverse_one, pieces, packed, context, scaled_two, inverse_two, kept_chunks = kept
    slots, features = upstream.shape
    wide, narrow = lax.axis_size("wide"), lax.axis_size("narrow")
    mixer_gap = (mixer[:, 0].astype(F32) - mixer[:, 1].astype(F32))[None]
    across, beside = wide_pieces(low(upstream))
    chunks = chunks_of(wide)
    merged, sums = [], []
    for chunk, select, saved in zip(chunks, selects, kept_chunks):
        rows, mixing, expert_rows, expert_pre, expert_act, pre, act = saved
        grads = wide_join(across, beside, chunk)
        expert_grads = to_experts(select, grads, slices)
        expert_mixing = jax.nn.softmax(
            jnp.dot(expert_rows, mixer, preferred_element_type=F32), axis=-1
        )
        through = product(expert_grads, expert_down, 1, 1)
        expert_dot = jnp.sum(expert_act.astype(F32) * through, axis=1, keepdims=True)
        expert_logit = -expert_mixing[:, :1] * expert_mixing[:, 1:] * expert_dot
        expert_grad_pre = low(activation_back(expert_pre, expert_mixing[:, 1:] * through))
        expert_back = product(expert_grad_pre, expert_up, 1, 1) + expert_logit * mixer_gap
        through = product(grads, down, 1, 1)
        dense_dot = jnp.sum(act.astype(F32) * through, axis=1, keepdims=True)
        dense_logit = mixing[:, :1] * mixing[:, 1:] * dense_dot
        grad_pre = low(activation_back(pre, mixing[:, :1] * through))
        dense_back = product(grad_pre, up, 1, 1) + dense_logit * mixer_gap
        merged.append(dense_back + from_experts(select, expert_back, slices))
        sums.append(
            (
                product(rows, grad_pre, 0, 0),
                product(act, low(mixing[:, :1] * grads.astype(F32)), 0, 0),
                product(expert_rows, expert_grad_pre, 0, 0),
                product(expert_act, low(expert_mixing[:, 1:] * expert_grads.astype(F32)), 0, 0),
                jnp.sum(rows.astype(F32) * dense_logit, axis=0)
                + jnp.sum(expert_rows.astype(F32) * expert_logit, axis=0),
            )
        )
    grad_second = wide_sums(chunks, merged, slots)
    grad_up, grad_down, grad_expert_up, grad_expert_down, grad_gap = [sum(s[1:], s[0]) for s in zip(*sums)]
    grad_up = narrow_sum(grad_up, 0)
    grad_down = narrow_sum(grad_down, 1)
    grad_norm_part, grad_norm_second = norm_back(grad_second, scaled_two, inverse_two, norm_second)
    grad_middle = upstream + grad_norm_part
    grad_attended = low(grad_middle)
    grad_contexts = split_columns(product(grad_attended, attention_out, 1, 1), narrow, at_narrow)
    grad_contexts = [grad_contexts[0]] + [
        swap(grad_contexts[j], "narrow", j) for j in range(1, narrow)
    ]
    grad_out = product(context, grad_attended, 0, 0)
    grad_out = narrow_sum(scatter_halves(*split_halves(grad_out, wide, at_wide)), 0)
    grad_in, parts = attention_back(pieces, attention_in, packed, grad_contexts, lengths)
    grad_in = low(scatter_halves(*split_halves(grad_in, wide, at_wide)))
    grad_in = pack_rows(
        [grad_in] + [swap(grad_in, "narrow", j) for j in range(1, narrow)], at_narrow
    )
    grad_in = jnp.transpose(grad_in.reshape(narrow, features // wide, 3, -1), (1, 2, 0, 3))
    grad_in = grad_in.reshape(features // wide, -1).astype(F32)
    grad_normed = parts[0].astype(F32)
    for j in range(1, narrow):
        grad_normed = grad_normed + swap(parts[j], "narrow", j).astype(F32)
    grad_norm_part, grad_norm_first = norm_back(grad_normed, scaled_one, inverse_one, norm_first)
    return grad_middle + grad_norm_part, (
        grad_in, grad_out, grad_up, grad_down, grad_expert_up[None], grad_expert_down[None],
        grad_norm_first, grad_norm_second, grad_gap,
    )


def narrow_slice(attention_in):
    rows, triple = attention_in.shape
    narrow = lax.axis_size("narrow")
    split = attention_in.reshape(rows, 3, narrow, triple // (3 * narrow))
    own = lax.dynamic_index_in_dim(split, lax.axis_index("narrow"), axis=2, keepdims=False)
    return own.reshape(rows, -1)


def gather_wide(own, at_wide):
    across, beside = wide_pieces(own)
    return pack_rows([p for pair in zip(across, beside) for p in pair], at_wide)


def body(
    inputs, cotangent, seq_len, shallow_routes, deep_routes,
    shallow_norm_first, shallow_attention_in, shallow_attention_out, shallow_norm_second,
    shallow_dense_up, shallow_dense_down, shallow_mixer, shallow_expert_up, shallow_expert_down,
    deep_norm_first, deep_attention_in, deep_attention_out, deep_norm_second,
    deep_dense_up, deep_dense_down, deep_mixer, deep_expert_up, deep_expert_down,
):
    wide, narrow = lax.axis_size("wide"), lax.axis_size("narrow")
    wide_at, narrow_at = lax.axis_index("wide"), lax.axis_index("narrow")
    at_wide, at_narrow = wide_at.reshape(1), narrow_at.reshape(1)
    slots, features = inputs.shape
    small = jnp.stack(
        [
            shallow_norm_first, shallow_norm_second, deep_norm_first, deep_norm_second,
            shallow_mixer[:, 0], shallow_mixer[:, 1], deep_mixer[:, 0], deep_mixer[:, 1],
        ]
    )
    small = jnp.transpose(gather_wide(small, at_wide).reshape(wide, 8, -1), (1, 0, 2)).reshape(8, features)
    gains = small[:4].astype(F32)
    lengths = seq_len[wide_at * narrow + (narrow_at ^ jnp.arange(narrow))]

    def selects_of(routes, slices):
        table = routes.reshape(wide, narrow, slots)
        own = lax.dynamic_index_in_dim(table, narrow_at, axis=1, keepdims=False)
        capacity = slices * max(1, 3 * slots // (2 * wide * narrow))
        groups = narrow // slices
        experts = [wide_at * groups + ((narrow_at // slices) ^ r) for r in range(groups)]
        return [
            place(own[wide_at ^ jnp.array(chunk_order(chunk))], experts, capacity)
            for chunk in chunks_of(wide)
        ]

    shallow_selects = selects_of(shallow_routes, SLICES_SHALLOW)
    deep_selects = selects_of(deep_routes, SLICES_DEEP)
    shallow = (
        gains[0], gather_wide(narrow_slice(shallow_attention_in), at_wide),
        gather_wide(shallow_attention_out, at_wide), gains[1], small[4:6].T,
        shallow_dense_up, shallow_dense_down, shallow_expert_up[0], shallow_expert_down[0],
    )
    deep = (
        gains[2], gather_wide(narrow_slice(deep_attention_in), at_wide),
        gather_wide(deep_attention_out, at_wide), gains[3], small[6:8].T,
        deep_dense_up, deep_dense_down, deep_expert_up[0], deep_expert_down[0],
    )
    passed, kept_shallow = layer_forward(
        inputs.astype(F32), shallow, shallow_selects, lengths, at_narrow, SLICES_SHALLOW
    )
    output, kept_deep = layer_forward(passed, deep, deep_selects, lengths, at_narrow, SLICES_DEEP)
    grad_passed, grads_deep = layer_backward(
        cotangent.astype(F32), kept_deep, deep, deep_selects, lengths, at_narrow, at_wide, SLICES_DEEP
    )
    grad_inputs, grads_shallow = layer_backward(
        grad_passed, kept_shallow, shallow, shallow_selects, lengths, at_narrow, at_wide, SLICES_SHALLOW
    )
    vectors = everywhere_sum(
        jnp.stack(list(grads_shallow[6:9]) + list(grads_deep[6:9]))
    )
    vectors = lax.dynamic_slice_in_dim(vectors, wide_at * (features // wide), features // wide, axis=1)

    def outputs_of(grads, rows):
        grad_mixer = jnp.stack([rows[2], -rows[2]], axis=1)
        return (
            rows[0], grads[0], grads[1], rows[1], grads[2], grads[3], grad_mixer, grads[4], grads[5],
        )

    return (
        (low(output), grad_inputs)
        + outputs_of(grads_shallow, vectors[:3])
        + outputs_of(grads_deep, vectors[3:])
    )


def solution(mesh):
    both = ("wide", "narrow")
    parameters = (
        P("wide"), P("wide", None), P("wide", None), P("wide"), P(None, "wide"),
        P("wide", None), P("wide", None), P(both, None, None), P(both, None, None),
    )
    return jax.shard_map(
        body,
        mesh=mesh,
        in_specs=(P(both, None), P(both, None), P(), P(), P()) + parameters + parameters,
        out_specs=(P(both, None), P(both, None)) + parameters + parameters,
        check_vma=False,
    )
```

```python
import jax
import jax.numpy as jnp
from jax import lax
from jax.experimental import pallas as pl
from jax.experimental.pallas import tpu as pltpu
from jax.sharding import PartitionSpec as P

HEAD_DIM = 64
SLICES_SHALLOW = 4
SLICES_DEEP = 2
F32 = jnp.float32
LOW = jnp.bfloat16
VMEM_LIMIT = 60 * 1024 * 1024


def low(value):
    return value.astype(LOW)


def swap(array, axis, distance):
    return lax.ppermute(array, axis, [(i, i ^ distance) for i in range(lax.axis_size(axis))])


def product(left, right, left_dim, right_dim):
    return lax.dot_general(
        left, right, (((left_dim,), (right_dim,)), ((), ())), preferred_element_type=F32
    )


def vmem():
    return pl.BlockSpec(memory_space=pltpu.VMEM)


def smem():
    return pl.BlockSpec(memory_space=pltpu.SMEM)


def call(kernel, outs, scalars, arrays, scratch=(), flops=0):
    moved = sum(a.size * a.dtype.itemsize for a in list(arrays) + list(outs))
    return pl.pallas_call(
        kernel,
        out_shape=tuple(outs),
        in_specs=[smem()] * len(scalars) + [vmem()] * len(arrays),
        out_specs=tuple(vmem() for _ in outs),
        scratch_shapes=list(scratch),
        compiler_params=pltpu.CompilerParams(vmem_limit_bytes=VMEM_LIMIT),
        cost_estimate=pl.CostEstimate(flops=flops, bytes_accessed=moved, transcendentals=0),
    )(*scalars, *arrays)


def shape(dims, kind):
    return jax.ShapeDtypeStruct(dims, kind)


def join_rows(pieces):
    if len(pieces) == 1:
        return pieces[0]
    count, (rows, columns) = len(pieces), pieces[0].shape

    def kernel(*refs):
        for k in range(count):
            refs[count][k * rows : (k + 1) * rows, :] = refs[k][...]

    return call(kernel, [shape((count * rows, columns), pieces[0].dtype)], [], pieces)[0]


def pack_columns(pieces, base):
    count, (rows, columns) = len(pieces), pieces[0].shape

    def kernel(base_ref, *refs):
        for k in range(count):
            start = pl.multiple_of((base_ref[0] ^ k) * columns, columns)
            refs[count][:, pl.ds(start, columns)] = refs[k][...]

    return call(kernel, [shape((rows, count * columns), pieces[0].dtype)], [base], pieces)[0]


def split_columns(whole, count, base):
    rows, columns = whole.shape[0], whole.shape[1] // count

    def kernel(base_ref, whole_ref, *outs):
        for k in range(count):
            start = pl.multiple_of((base_ref[0] ^ k) * columns, columns)
            outs[k][...] = low(whole_ref[:, pl.ds(start, columns)])

    return call(kernel, [shape((rows, columns), LOW)] * count, [base], [whole])


def own_slab(attention_in, extra, base, below):
    rows, triple = attention_in.shape
    columns = triple // (3 * lax.axis_size("narrow"))
    below_rows = below.shape[0] if below is not None else 0
    wide_extra = extra.shape[1] if extra is not None else 0

    def kernel(base_ref, weight_ref, *refs):
        refs, out = list(refs[:-1]), refs[-1]
        for part in range(3):
            start = pl.multiple_of(part * (triple // 3) + base_ref[0] * columns, columns)
            out[:rows, part * columns : (part + 1) * columns] = weight_ref[:, pl.ds(start, columns)]
        if extra is not None:
            out[:rows, 3 * columns :] = refs.pop(0)[...]
        if below is not None:
            out[rows:, :] = jnp.zeros((below_rows, 3 * columns + wide_extra), LOW)
            out[rows:, : below.shape[1]] = refs.pop(0)[...]

    arrays = [attention_in] + [a for a in (extra, below) if a is not None]
    outs = [shape((rows + below_rows, 3 * columns + wide_extra), LOW)]
    return call(kernel, outs, [base], arrays)[0]


def join_slab(found, rows, parts, at_wide, below=0):
    across, beside = found
    pieces = [p for pair in zip(across, beside) for p in pair]
    count = len(pieces)

    def kernel(base_ref, *refs):
        for k in range(count):
            start = pl.multiple_of((base_ref[0] ^ k) * rows, rows)
            at = 0
            for i, columns in enumerate(parts):
                refs[count + i][pl.ds(start, rows), :] = refs[k][:rows, at : at + columns]
                at += columns
            if below:
                start = pl.multiple_of((base_ref[0] ^ k) * below, below)
                refs[-1][pl.ds(start, below), :] = refs[k][rows:, :rows]

    outs = [shape((count * rows, columns), LOW) for columns in parts]
    if below:
        outs.append(shape((count * below, rows), LOW))
    return call(kernel, outs, [at_wide], pieces)


def spread_columns(pieces, base):
    count, (rows, triple) = len(pieces), pieces[0].shape
    columns = triple // 3

    def kernel(base_ref, *refs):
        for k in range(count):
            for part in range(3):
                start = part * count * columns + (base_ref[0] ^ k) * columns
                refs[count][:, pl.ds(pl.multiple_of(start, columns), columns)] = refs[k][
                    :, part * columns : (part + 1) * columns
                ].astype(F32)

    return call(kernel, [shape((rows, count * triple), F32)], [base], pieces)[0]


def narrow_join(own, at_narrow):
    narrow = lax.axis_size("narrow")
    return spread_columns(
        [own] + [swap(own, "narrow", j) for j in range(1, narrow)], at_narrow
    )


def reorder(whole, slots, at_wide, outward):
    count = whole.shape[0] // slots
    order = list(range(0, count, 2)) + list(range(1, count, 2))

    def kernel(base_ref, whole_ref, out_ref):
        for i, k in enumerate(order):
            start = pl.multiple_of((base_ref[0] ^ k) * slots, slots)
            if outward:
                out_ref[pl.ds(start, slots), :] = whole_ref[i * slots : (i + 1) * slots, :]
            else:
                out_ref[i * slots : (i + 1) * slots, :] = whole_ref[pl.ds(start, slots), :]

    return call(kernel, [shape(whole.shape, whole.dtype)], [at_wide], [whole])[0]


def outer_pair(pieces, grad_packed, context, grad_attended):
    count, (slots, features) = len(pieces), pieces[0].shape
    columns = grad_packed.shape[1]

    def kernel(*refs):
        left = jnp.concatenate([r[...] for r in refs[:count]], axis=0)
        packed_ref, context_ref, attended_ref, out = refs[count:]
        out[:, :columns] = low(product(left, packed_ref[...], 0, 0))
        out[:, columns:] = low(product(context_ref[...], attended_ref[...], 0, 0))

    outs = [shape((features, columns + context.shape[1]), LOW)]
    flops = 2 * slots * features * (count * columns + context.shape[1])
    arrays = list(pieces) + [grad_packed, context, grad_attended]
    return call(kernel, outs, [], arrays, flops=flops)[0]


def join_pair(gathered, columns):
    narrow = lax.axis_size("narrow")
    rows = gathered.shape[0] // narrow
    features = gathered.shape[1] - columns
    third = columns // 3

    def kernel(whole_ref, in_ref, out_ref):
        total = None
        for j in range(narrow):
            block = whole_ref[j * rows : (j + 1) * rows, :]
            for part in range(3):
                at = part * narrow * third + j * third
                in_ref[:, at : at + third] = block[:, part * third : (part + 1) * third].astype(F32)
            found = block[:, columns:].astype(F32)
            total = found if total is None else total + found
        out_ref[...] = total

    outs = [shape((rows, narrow * columns), F32), shape((rows, features), F32)]
    return call(kernel, outs, [], [gathered])


def dense_products(parts):
    return low(up_product(parts)), low(down_product(parts))


def narrow_step(pair, step):
    bits = lax.axis_size("narrow").bit_length() - 1
    return [
        low(value.astype(F32) + swap(value, "narrow", 1 << (step + i) % bits).astype(F32))
        for i, value in enumerate(pair)
    ]


def narrow_last(pair):
    bits = lax.axis_size("narrow").bit_length() - 1
    for step in range(1, bits - 1):
        pair = narrow_step(pair, step)
    return [
        (value, swap(value, "narrow", 1 << (bits - 1 + i) % bits)) for i, value in enumerate(pair)
    ]


def dense_join(parts):
    up, down = parts
    features, units = up.shape
    fold = features // units

    def kernel(up_ref, down_ref, out_ref):
        for i in range(fold):
            out_ref[:units, i * units : (i + 1) * units] = up_ref[i * units : (i + 1) * units, :]
        out_ref[units:, :] = down_ref[...]

    return call(kernel, [shape((2 * units, features), LOW)], [], [up, down])[0]


def narrow_scatter(whole):
    return lax.psum_scatter(whole, "narrow", scatter_dimension=0, tiled=True)


def narrow_gather(own):
    return lax.all_gather(own, "narrow", axis=0, tiled=True)


def dense_outputs(gathered):
    units, features = gathered.shape[0] // 2, gathered.shape[1]
    fold = features // units

    def kernel(whole_ref, up_ref, down_ref):
        for i in range(fold):
            up_ref[i * units : (i + 1) * units, :] = whole_ref[
                :units, i * units : (i + 1) * units
            ].astype(F32)
        down_ref[...] = whole_ref[units:, :].astype(F32)

    return call(kernel, [shape((features, units), F32), shape((units, features), F32)], [], [gathered])


def gather_wide(own):
    return lax.all_gather(own, "wide", axis=0, tiled=True)


def after(value, *others):
    return lax.optimization_barrier((value,) + others)[0]


def reversed_order(count):
    bits = count.bit_length() - 1
    return [sum((i >> b & 1) << (bits - 1 - b) for b in range(bits)) for i in range(count)]


def outer_halves(lefts, right, base):
    count = len(lefts)
    wide = lax.axis_size("wide")
    slots, features = lefts[0].shape
    columns = right.shape[1]
    rows = features // wide
    order = reversed_order(wide)

    def kernel(base_ref, *refs):
        right_ref, keep_ref, send_ref, total_ref = refs[count:]
        left = refs[0][...] if count == 1 else jnp.concatenate([r[...] for r in refs[:count]], axis=0)
        total_ref[...] = product(left, right_ref[...], 0, 0)
        for i, k in enumerate(order):
            start = pl.multiple_of((base_ref[0] ^ k) * rows, rows)
            out, at = (keep_ref, i) if i < wide // 2 else (send_ref, i - wide // 2)
            out[at * rows : (at + 1) * rows, :] = low(total_ref[pl.ds(start, rows), :])

    outs = [shape((features // 2, columns), LOW)] * 2
    scratch = [pltpu.VMEM((features, columns), F32)]
    flops = 2 * count * slots * features * columns
    return call(kernel, outs, [base], list(lefts) + [right], scratch, flops)


def pair_sum(own, received, slots):
    count = own.shape[0] // slots
    features = own.shape[1]

    def kernel(own_ref, received_ref, *outs):
        for k in range(count):
            at = slice(k * slots, (k + 1) * slots)
            total = own_ref[at, :] + received_ref[at, :].astype(F32)
            outs[k][...] = total if k == 0 else low(total)

    outs = [shape((slots, features), F32)] + [shape((slots, features), LOW)] * (count - 1)
    return call(kernel, outs, [], [own, received])


def halving_step(halves, distance):
    keep, send = halves
    total = keep.astype(F32) + swap(send, "wide", distance).astype(F32)
    if 2 * distance == lax.axis_size("wide"):
        return total
    half = total.shape[0] // 2
    return total[:half], low(total[half:])


def halving_rest(halves, distance):
    while distance < lax.axis_size("wide"):
        halves = halving_step(halves, distance)
        distance *= 2
    return halves


def together(value, other):
    return lax.optimization_barrier((value, other))


def narrow_sum(value, first):
    narrow = lax.axis_size("narrow")
    bits = narrow.bit_length() - 1
    for b in range(bits):
        value = value + swap(low(value), "narrow", 1 << (b + first) % bits).astype(F32)
    return value


def narrow_rest(value):
    distance = 2
    while distance < lax.axis_size("narrow"):
        value = value + swap(low(value), "narrow", distance).astype(F32)
        distance *= 2
    return value


def everywhere_sum(value):
    for axis in ("narrow", "wide"):
        distance = 1
        while distance < lax.axis_size(axis):
            value = value + swap(value, axis, distance)
            distance *= 2
    return value


def layer_norm(source, gain):
    centre = source - jnp.mean(source, axis=-1, keepdims=True)
    inverse = lax.rsqrt(jnp.mean(centre * centre, axis=-1, keepdims=True) + 1e-05)
    scaled = centre * inverse
    return scaled * gain, scaled, inverse


def norm_back(upstream, scaled, inverse, gain):
    grad_scaled = upstream * gain
    mean_first = jnp.mean(grad_scaled, axis=-1, keepdims=True)
    mean_second = jnp.mean(grad_scaled * scaled, axis=-1, keepdims=True)
    return (
        inverse * (grad_scaled - mean_first - scaled * mean_second),
        jnp.sum(upstream * scaled, axis=0),
    )


def activate(source):
    return jax.nn.gelu(source)


def activation_back(source, upstream):
    return jax.vjp(activate, source)[1](upstream)[0]


def softened_scores(queries, keys, allowed):
    scores = product(queries, keys, 1, 1) * HEAD_DIM ** (-0.5)
    scores = jnp.where(allowed, scores, -1e30)
    raised = jnp.exp(scores - jnp.max(scores, axis=-1, keepdims=True))
    return raised / jnp.sum(raised, axis=-1, keepdims=True)


def allowed_of(length, slots):
    rows_at = lax.broadcasted_iota(jnp.int32, (slots, slots), 0)
    cols_at = lax.broadcasted_iota(jnp.int32, (slots, slots), 1)
    return (cols_at <= rows_at) & (cols_at < length)


def head_parts(packed, head, columns):
    return [
        packed[:, part * columns + head * HEAD_DIM : part * columns + (head + 1) * HEAD_DIM]
        for part in range(3)
    ]


def attention(pieces, gain, weight, lengths):
    count, (slots, features) = len(pieces), pieces[0].shape
    columns = weight.shape[1] // 3
    raw = gain is not None

    def kernel(lengths_ref, *refs):
        ins, weight_ref, refs = refs[:count], refs[count], refs[count + 1 :]
        if raw:
            gain_ref, refs = refs[0], refs[1:]
        packed_ref, outs = refs[0], refs[1 : count + 1]
        for j in range(count):
            if raw:
                rows = low(layer_norm(ins[j][...].astype(F32), gain_ref[...])[0])
                refs[count + 1 + j][...] = rows
            else:
                rows = ins[j][...]
            packed = low(product(rows, weight_ref[...], 1, 0))
            packed_ref[j] = packed
            allowed = allowed_of(lengths_ref[j], slots)
            found = []
            for head in range(columns // HEAD_DIM):
                queries, keys, values = head_parts(packed, head, columns)
                softened = softened_scores(queries, keys, allowed)
                found.append(product(low(softened), values, 1, 0))
            outs[j][...] = low(jnp.concatenate(found, axis=1))

    outs = [shape((count, slots, 3 * columns), LOW)] + [shape((slots, columns), LOW)] * count
    arrays = list(pieces) + [weight]
    if raw:
        outs += [shape((slots, features), LOW)] * count
        arrays.append(gain[None])
    flops = 2 * count * slots * features * 3 * columns
    packed, *found = call(kernel, outs, [lengths], arrays, flops=flops)
    return packed, found[:count], found[count:] if raw else pieces


def attention_back(packed, grads, lengths):
    count, (slots, columns) = len(grads), grads[0].shape
    scaling = HEAD_DIM ** (-0.5)

    def kernel(lengths_ref, packed_ref, *refs):
        out = refs[count]
        for j in range(count):
            allowed = allowed_of(lengths_ref[j], slots)
            whole = packed_ref[j]
            grad_whole = refs[j][...]
            found = [[], [], []]
            for head in range(columns // HEAD_DIM):
                queries, keys, values = head_parts(whole, head, columns)
                grad_head = grad_whole[:, head * HEAD_DIM : (head + 1) * HEAD_DIM]
                softened = softened_scores(queries, keys, allowed)
                grad_soft = product(grad_head, values, 1, 1)
                inner = jnp.sum(softened * grad_soft, axis=-1, keepdims=True)
                grad_scores = low(softened * (grad_soft - inner))
                found[0].append(scaling * product(grad_scores, keys, 1, 0))
                found[1].append(scaling * product(grad_scores, queries, 0, 0))
                found[2].append(product(low(softened), grad_head, 0, 0))
            out[j * slots : (j + 1) * slots, :] = low(
                jnp.concatenate(found[0] + found[1] + found[2], axis=1)
            )

    outs = [shape((count * slots, 3 * columns), LOW)]
    return call(kernel, outs, [lengths], [packed] + list(grads))[0]


def normed_back(grad_packed, weight, count):
    slots, features = grad_packed.shape[0] // count, weight.shape[0]

    def kernel(grad_ref, weight_ref, *outs):
        whole = low(product(grad_ref[...], weight_ref[...], 1, 1))
        for j in range(count):
            outs[j][...] = whole[j * slots : (j + 1) * slots]

    outs = [shape((slots, features), LOW)] * count
    flops = 2 * count * slots * features * weight.shape[1]
    return call(kernel, outs, [], [grad_packed, weight], flops=flops)


def wide_across(own):
    return [own] + [swap(own, "wide", apart) for apart in range(2, lax.axis_size("wide"), 2)]


def wide_pieces(own):
    across = wide_across(own)
    return across, [swap(piece, "wide", 1) for piece in across]


def wide_join(pieces):
    across, beside = pieces
    return join_rows(list(across) + list(beside))


def wide_sends(own, received, slots):
    parts = pair_sum(own, received, slots)
    return [parts[0]] + [swap(p, "wide", 2 * (i + 1)) for i, p in enumerate(parts[1:])]


def wide_total(parts):
    total = parts[0]
    for part in parts[1:]:
        total = total + part.astype(F32)
    return total


def wide_sums(halves, slots):
    own, other = halves
    return wide_total(wide_sends(own, swap(other, "wide", 1), slots))


def place(labels, experts, capacity):
    blocks, slots = labels.shape
    first = jnp.arange(blocks, dtype=jnp.int32)[:, None] * capacity - 1
    places = jnp.arange(blocks * capacity, dtype=jnp.int32)
    selects = []
    for expert in experts:
        chosen = labels == expert
        at = jnp.where(chosen, first + jnp.cumsum(chosen.astype(jnp.int32), axis=1), -1)
        selects.append(low(places[:, None] == at.reshape(-1)[None, :]))
    return selects


def picked(selects, rows):
    return [low(product(select, rows, 1, 0)) for select in selects]


def exchanged(sent, slices):
    narrow = lax.axis_size("narrow")
    return join_rows(
        [sent[j // slices] if j == 0 else swap(sent[j // slices], "narrow", j) for j in range(narrow)]
    )


def to_experts(selects, rows, slices):
    return exchanged(picked(selects, rows), slices)


def from_experts(selects, outcome, slices):
    narrow = lax.axis_size("narrow")
    parts = outcome.reshape(narrow, -1, outcome.shape[-1])
    found = []
    for r in range(len(selects)):
        total = None
        for j in range(r * slices, (r + 1) * slices):
            part = parts[j] if j == 0 else swap(low(parts[j]), "narrow", j).astype(F32)
            total = part if total is None else total + part
        found.append(low(total))
    return found


def spread_of(selects, found, at):
    total = None
    for select, rows in zip(selects, found):
        part = product(select[:, at], rows, 0, 0)
        total = part if total is None else total + part
    return total


def layer_forward(source, raw, weights, selects, lengths, at_narrow, slices, first_work=None, second_work=None):
    norm_first, attention_in, attention_out, norm_second, mixer, up, down, expert_up, expert_down = weights
    slots, features = source.shape
    wide, narrow = lax.axis_size("wide"), lax.axis_size("narrow")
    normed, scaled_one, inverse_one = layer_norm(source, norm_first)
    own = low(normed)
    pieces = raw
    if raw is None:
        pieces = [own] + [swap(own, "narrow", j) for j in range(1, narrow)]
    if first_work is not None:
        pieces, first_found = together(pieces, first_work(own))
    packed, contexts, pieces = attention(
        pieces, None if raw is None else norm_first, attention_in, lengths
    )
    context = pack_columns(
        [contexts[0]] + [swap(contexts[j], "narrow", j) for j in range(1, narrow)], at_narrow
    )
    middle = source + jnp.dot(context, attention_out, preferred_element_type=F32)
    second, scaled_two, inverse_two = layer_norm(middle, norm_second)
    second = low(second)
    across, beside = wide_pieces(second)
    if second_work is not None:
        across, second_found = together(across, second_work(second, first_found))
    rows = wide_join((across, beside))
    mixing = jax.nn.softmax(jnp.dot(rows, mixer, preferred_element_type=F32), axis=-1)
    pre = jnp.dot(rows, up, preferred_element_type=F32)
    act = low(activate(pre))
    expert_rows, (mixing, pre, act) = together(
        to_experts(selects, rows, slices), (mixing, pre, act)
    )
    expert_pre = jnp.dot(expert_rows, expert_up, preferred_element_type=F32)
    expert_act = low(activate(expert_pre))
    kept = (
        scaled_one, inverse_one, pieces, packed, context, scaled_two, inverse_two,
        (rows, mixing, expert_rows, expert_pre, expert_act, pre, act),
    )
    return (middle, kept) if second_work is None else (middle, kept, second_found)


def experts_found(kept, weights, selects, slices, gate=None):
    act = kept[7][4] if gate is None else after(kept[7][4], gate)
    outcome = jnp.dot(act, weights[8], preferred_element_type=F32)
    return from_experts(selects, outcome, slices)


def merged_halves(kept, weights, selects, found, slots):
    mixing, act = kept[7][1], kept[7][6]

    def merged(at):
        dense = jnp.dot(act[at], weights[6], preferred_element_type=F32)
        return mixing[at, :1] * dense + mixing[at, 1:] * spread_of(selects, found, at)

    half = act.shape[0] // 2
    return merged(slice(0, half)), low(merged(slice(half, 2 * half)))


def dense_back_of(through, kept, weights):
    rows, mixing, _, _, _, pre, act = kept[7]
    dense_dot = jnp.sum(act.astype(F32) * through, axis=1, keepdims=True)
    dense_logit = mixing[:, :1] * mixing[:, 1:] * dense_dot
    grad_pre = low(activation_back(pre, mixing[:, :1] * through))
    return grad_pre, dense_logit


def experts_back(upstream, gathered, kept, weights, selects, slices, beneath, alongside):
    norm_second, mixer, up, down, expert_up, expert_down = weights[3:]
    scaled_two, inverse_two = kept[5:7]
    rows, mixing, expert_rows, expert_pre, expert_act, pre, act = kept[7]
    slots = upstream.shape[0]
    wide = lax.axis_size("wide")
    mixer_gap = (mixer[:, 0].astype(F32) - mixer[:, 1].astype(F32))[None]
    grads, expert_grads, through, (grad_pre, dense_logit) = gathered
    expert_mixing = jax.nn.softmax(
        jnp.dot(expert_rows, mixer, preferred_element_type=F32), axis=-1
    )
    expert_dot = jnp.sum(expert_act.astype(F32) * through, axis=1, keepdims=True)
    expert_logit = -expert_mixing[:, :1] * expert_mixing[:, 1:] * expert_dot
    expert_grad_pre = low(activation_back(expert_pre, expert_mixing[:, 1:] * through))
    expert_back = product(expert_grad_pre, expert_up, 1, 1) + expert_logit * mixer_gap
    dense = (rows, grad_pre, act, mixing[:, :1], grads)
    found = from_experts(selects, expert_back, slices)
    experts = (
        expert_rows, expert_grad_pre,
        expert_act, expert_mixing[:, 1:], expert_grads,
    )
    found, beneath_found = together(found, beneath(expert_back, experts, dense))

    def merged(at):
        dense_back = product(grad_pre[at], up, 1, 1) + dense_logit[at] * mixer_gap
        return dense_back + spread_of(selects, found, at)

    half = grad_pre.shape[0] // 2
    halves = merged(slice(0, half)), low(merged(slice(half, 2 * half)))
    grad_gap = jnp.sum(rows.astype(F32) * dense_logit, axis=0) + jnp.sum(
        expert_rows.astype(F32) * expert_logit, axis=0
    )
    parts = wide_sends(halves[0], swap(halves[1], "wide", 1), slots)
    grad_second, alongside_found = together(
        wide_total(parts), alongside(parts[0], beneath_found, experts, dense)
    )
    grad_norm_part, grad_norm_second = norm_back(grad_second, scaled_two, inverse_two, norm_second)
    return (
        upstream + grad_norm_part, dense, experts, (grad_norm_second, grad_gap),
        beneath_found, alongside_found,
    )


def up_product(parts):
    return product(parts[0], parts[1], 0, 0)


def down_product(parts):
    act, mix, grads = parts[2:]
    return product(act, low(mix * grads.astype(F32)), 0, 0)


def attention_grads(grad_middle, kept, weights, lengths, at_narrow, at_wide, last, hold, aside=None):
    norm_first, attention_in, attention_out = weights[:3]
    scaled_one, inverse_one, pieces, packed, context = kept[:5]
    narrow = lax.axis_size("narrow")
    grad_attended = low(grad_middle)
    grad_contexts = split_columns(product(grad_attended, attention_out, 1, 1), narrow, at_narrow)
    grad_contexts = [grad_contexts[0]] + [
        swap(grad_contexts[j], "narrow", j) for j in range(1, narrow)
    ]
    if last:
        out_halves = outer_halves([context], after(grad_attended, grad_contexts[0]), at_wide)
        grad_contexts, out_halves = together(grad_contexts, halving_step(out_halves, 1))
        out_halves = halving_step(out_halves, 2)
        aside = aside(grad_contexts)
    grad_packed = attention_back(packed, grad_contexts, lengths)
    if last:
        grad_packed, out_halves = together(grad_packed, out_halves)
        in_halves = outer_halves(pieces, grad_packed, at_wide)
        parts = normed_back(after(grad_packed, in_halves), attention_in, narrow)
        in_halves = halving_step(in_halves, 1)
        gate = in_halves
        in_halves = halving_step(in_halves, 2)
        in_sum = low(halving_rest(in_halves, 4))
        out_sum = halving_rest(out_halves, 4)
        out_sum = after(out_sum, in_halves) + swap(
            low(after(out_sum, in_halves)), "narrow", 1
        ).astype(F32)
        out_sum = narrow_rest(after(out_sum, in_sum))
        weight_grads = narrow_join(in_sum, at_narrow), out_sum
        hold = hold, in_sum, aside
    else:
        grad_packed, hold = together(grad_packed, hold)
        parts = normed_back(grad_packed, attention_in, narrow)
        weight_grads = (pieces, after(grad_packed, parts), context, grad_attended)
    parts = [parts[0]] + [swap(parts[j], "narrow", j) for j in range(1, narrow)]
    grad_normed = sum(part.astype(F32) for part in (after(parts, gate) if last else parts))
    grad_norm_part, grad_norm_first = norm_back(grad_normed, scaled_one, inverse_one, norm_first)
    return grad_middle + grad_norm_part, grad_norm_first, weight_grads, hold


def body(
    inputs, cotangent, seq_len, shallow_routes, deep_routes,
    shallow_norm_first, shallow_attention_in, shallow_attention_out, shallow_norm_second,
    shallow_dense_up, shallow_dense_down, shallow_mixer, shallow_expert_up, shallow_expert_down,
    deep_norm_first, deep_attention_in, deep_attention_out, deep_norm_second,
    deep_dense_up, deep_dense_down, deep_mixer, deep_expert_up, deep_expert_down,
):
    wide, narrow = lax.axis_size("wide"), lax.axis_size("narrow")
    wide_at, narrow_at = lax.axis_index("wide"), lax.axis_index("narrow")
    at_wide, at_narrow = wide_at.reshape(1), narrow_at.reshape(1)
    slots, features = inputs.shape
    small = jnp.stack(
        [
            shallow_norm_first, shallow_norm_second, deep_norm_first, deep_norm_second,
            shallow_mixer[:, 0], shallow_mixer[:, 1], deep_mixer[:, 0], deep_mixer[:, 1],
        ]
    )
    narrow_columns = 3 * features // narrow
    rows_own = shallow_attention_in.shape[0]
    input_pieces = [inputs] + [swap(inputs, "narrow", j) for j in range(1, narrow)]
    across = wide_across(own_slab(shallow_attention_in, None, at_narrow, small))
    lengths = seq_len[wide_at * narrow + (narrow_at ^ jnp.arange(narrow))]
    deep_slab = own_slab(deep_attention_in, None, at_narrow, None)
    across, (input_pieces, lengths, deep_slab) = together(
        across, (input_pieces, lengths, deep_slab)
    )
    in_pieces = across, [swap(piece, "wide", 1) for piece in across]
    shallow_in, small = join_slab(
        in_pieces, rows_own, [narrow_columns], at_wide, small.shape[0]
    )
    shallow_out = gather_wide(after(shallow_attention_out, in_pieces[0][-1]))
    small = jnp.transpose(small.reshape(wide, 8, -1), (1, 0, 2)).reshape(8, features)
    gains = small[:4].astype(F32)
    def selects_of(routes, slices):
        table = routes.reshape(wide, narrow, slots)
        own = lax.dynamic_index_in_dim(table, narrow_at, axis=1, keepdims=False)
        capacity = slices * max(1, 3 * slots // (2 * wide * narrow))
        groups = narrow // slices
        experts = [wide_at * groups + ((narrow_at // slices) ^ r) for r in range(groups)]
        order = jnp.array(list(range(0, wide, 2)) + list(range(1, wide, 2)))
        return place(own[wide_at ^ order], experts, capacity)

    shallow_selects = selects_of(shallow_routes, SLICES_SHALLOW)
    deep_selects = selects_of(deep_routes, SLICES_DEEP)
    shallow = (
        gains[0], shallow_in, shallow_out, gains[1], small[4:6].T,
        shallow_dense_up, shallow_dense_down, shallow_expert_up[0], shallow_expert_down[0],
    )
    middle, kept_shallow = layer_forward(
        inputs.astype(F32), input_pieces, shallow, shallow_selects, lengths, at_narrow, SLICES_SHALLOW
    )
    deep_in = gather_wide(after(deep_slab, kept_shallow[7][0]))
    all_grads = gather_wide(after(cotangent, kept_shallow[7][2]))
    found = experts_found(kept_shallow, shallow, shallow_selects, SLICES_SHALLOW)
    halves = merged_halves(kept_shallow, shallow, shallow_selects, found, slots)
    total = wide_sums(halves, slots)
    passed = middle + total
    deep_out = gather_wide(after(deep_attention_out, total))
    deep = (
        gains[2], deep_in, deep_out, gains[3], small[6:8].T,
        deep_dense_up, deep_dense_down, deep_expert_up[0], deep_expert_down[0],
    )
    def first_work(own):
        grads = reorder(after(all_grads, own), slots, at_wide, False)
        return grads, picked(deep_selects, grads)

    def second_work(second, found):
        grads, sent = found
        expert_grads = exchanged(after(sent, second), SLICES_DEEP)
        return (
            grads, expert_grads, product(after(grads, second), deep_dense_down, 1, 1),
            product(expert_grads, deep_expert_down[0], 1, 1),
        )

    middle, kept_deep, gathered = layer_forward(
        passed, None, deep, deep_selects, lengths, at_narrow, SLICES_DEEP, first_work, second_work
    )
    grad_middle, _, deep_experts, deep_rows, whole, (deep_down, token) = experts_back(
        cotangent.astype(F32),
        gathered[:2] + (gathered[3], dense_back_of(gathered[2], kept_deep, deep)), kept_deep,
        deep, deep_selects, SLICES_DEEP,
        lambda token, experts, dense: dense_join(dense_products(dense)),
        lambda token, found, experts, dense: (down_product(after(experts, token)), token),
    )
    found = experts_found(kept_deep, deep, deep_selects, SLICES_DEEP, token)
    grad_passed, deep_first, outer_parts, (whole, found) = attention_grads(
        grad_middle, kept_deep, deep, lengths, at_narrow, at_wide, False,
        (narrow_scatter(whole), found),
    )
    passed_low = low(grad_passed)
    across, beside = wide_pieces(passed_low)
    halves = merged_halves(kept_deep, deep, deep_selects, after(found, passed_low), slots)
    result = reorder(
        jnp.concatenate([low(halves[0]), halves[1]], axis=0), slots, at_wide, True
    )
    deep_up = up_product(after(deep_experts, passed_low))
    across, (result, deep_up, whole) = together(across, (result, deep_up, narrow_gather(whole)))
    grads = wide_join((across, beside))
    pair = outer_pair(*after(outer_parts, grads))
    deep_dense = dense_outputs(after(whole, grads))
    expert_grads, (pair, deep_dense, dense_back) = together(
        to_experts(shallow_selects, grads, SLICES_SHALLOW),
        (
            pair, deep_dense,
            dense_back_of(product(grads, shallow_dense_down, 1, 1), kept_shallow, shallow),
        ),
    )
    pair = lax.psum_scatter(pair, "wide", scatter_dimension=0, tiled=True)

    grad_middle, _, _, shallow_rows, _, (shallow_experts, shallow_dense, pair) = experts_back(
        grad_passed,
        (grads, expert_grads, product(expert_grads, shallow_expert_down[0], 1, 1), dense_back),
        kept_shallow, shallow, shallow_selects, SLICES_SHALLOW,
        lambda token, experts, dense: dense_products(after(dense, token)),
        lambda token, found, experts, dense: (
            [f(after(experts, token)) for f in (up_product, down_product)],
            narrow_step(after(found, token), 0), pair,
        ),
    )
    shallow_up, shallow_down = shallow_experts
    total = lax.psum_scatter(
        after(result, grad_middle), "wide", scatter_dimension=0, tiled=True
    )
    grad_inputs, shallow_first, (grad_shallow_in, grad_shallow_out), total = attention_grads(
        grad_middle, kept_shallow, shallow, lengths, at_narrow, at_wide, True, total,
        lambda token: narrow_last(after(shallow_dense, token)),
    )
    total, vector_gate, shallow_dense = total
    shallow_dense, total, pair = after((shallow_dense, total, narrow_gather(pair)), vector_gate)
    shallow_dense = [own.astype(F32) + other.astype(F32) for own, other in shallow_dense]
    output = middle + total.astype(F32)
    grad_deep_in, grad_deep_out = join_pair(pair, narrow_columns)
    deep_up, deep_down = deep_up[None], deep_down[None]
    shallow_up, shallow_down = shallow_up[None], shallow_down[None]
    grads_shallow = (
        grad_shallow_in, grad_shallow_out, *shallow_dense, shallow_up, shallow_down,
        shallow_first, *shallow_rows,
    )
    grads_deep = (
        grad_deep_in, grad_deep_out, *deep_dense, deep_up, deep_down, deep_first, *deep_rows,
    )
    vectors = everywhere_sum(
        after(jnp.stack(list(grads_shallow[6:]) + list(grads_deep[6:])), vector_gate)
    )
    vectors = lax.dynamic_slice_in_dim(vectors, wide_at * (features // wide), features // wide, axis=1)

    def outputs_of(grads, rows):
        grad_mixer = jnp.stack([rows[2], -rows[2]], axis=1)
        return (
            rows[0], grads[0], grads[1], rows[1], grads[2], grads[3], grad_mixer, grads[4], grads[5],
        )

    return (
        (low(output), grad_inputs)
        + outputs_of(grads_shallow, vectors[:3])
        + outputs_of(grads_deep, vectors[3:])
    )


def solution(mesh):
    both = ("wide", "narrow")
    parameters = (
        P("wide"), P("wide", None), P("wide", None), P("wide"), P(None, "wide"),
        P("wide", None), P("wide", None), P(both, None, None), P(both, None, None),
    )
    return jax.shard_map(
        body,
        mesh=mesh,
        in_specs=(P(both, None), P(both, None), P(), P(), P()) + parameters + parameters,
        out_specs=(P(both, None), P(both, None)) + parameters + parameters,
        check_vma=False,
    )
```

```python
import jax
import jax.numpy as jnp
from jax import lax
from jax.experimental import pallas as pl
from jax.experimental.pallas import tpu as pltpu
from jax.sharding import PartitionSpec as P

HEAD_DIM = 64
SLICES_SHALLOW = 4
SLICES_DEEP = 2
F32 = jnp.float32
LOW = jnp.bfloat16
VMEM_LIMIT = 60 * 1024 * 1024


def low(value):
    return value.astype(LOW)


def swap(array, axis, distance):
    return lax.ppermute(array, axis, [(i, i ^ distance) for i in range(lax.axis_size(axis))])


def product(left, right, left_dim, right_dim):
    return lax.dot_general(
        left, right, (((left_dim,), (right_dim,)), ((), ())), preferred_element_type=F32
    )


def vmem():
    return pl.BlockSpec(memory_space=pltpu.VMEM)


def smem():
    return pl.BlockSpec(memory_space=pltpu.SMEM)


def call(kernel, outs, scalars, arrays, scratch=(), flops=0):
    moved = sum(a.size * a.dtype.itemsize for a in list(arrays) + list(outs))
    return pl.pallas_call(
        kernel,
        out_shape=tuple(outs),
        in_specs=[smem()] * len(scalars) + [vmem()] * len(arrays),
        out_specs=tuple(vmem() for _ in outs),
        scratch_shapes=list(scratch),
        compiler_params=pltpu.CompilerParams(vmem_limit_bytes=VMEM_LIMIT),
        cost_estimate=pl.CostEstimate(flops=flops, bytes_accessed=moved, transcendentals=0),
    )(*scalars, *arrays)


def shape(dims, kind):
    return jax.ShapeDtypeStruct(dims, kind)


def join_rows(pieces):
    if len(pieces) == 1:
        return pieces[0]
    count, (rows, columns) = len(pieces), pieces[0].shape

    def kernel(*refs):
        for k in range(count):
            refs[count][k * rows : (k + 1) * rows, :] = refs[k][...]

    return call(kernel, [shape((count * rows, columns), pieces[0].dtype)], [], pieces)[0]


def context_back(grads, weight, count, base):
    slots, features = grads.shape
    columns = features // count

    def kernel(base_ref, grads_ref, weight_ref, *outs):
        for k in range(count):
            start = pl.multiple_of((base_ref[0] ^ k) * columns, columns)
            outs[k][...] = low(product(grads_ref[...], weight_ref[pl.ds(start, columns), :], 1, 1))

    outs = [shape((slots, columns), LOW)] * count
    flops = 2 * slots * features * features
    return call(kernel, outs, [base], [grads, weight], flops=flops)


def attended(pieces, weight, source, gain, base):
    count, (slots, columns) = len(pieces), pieces[0].shape
    features = source.shape[1]

    def kernel(base_ref, weight_ref, source_ref, gain_ref, *refs):
        context_ref, middle_ref, second_ref, scaled_ref, inverse_ref = refs[count:]
        total = source_ref[...]
        for k in range(count):
            start = pl.multiple_of((base_ref[0] ^ k) * columns, columns)
            context_ref[:, pl.ds(start, columns)] = refs[k][...]
            total = total + product(refs[k][...], weight_ref[pl.ds(start, columns), :], 1, 0)
        middle_ref[...] = total
        second, scaled, inverse = layer_norm(total, gain_ref[...])
        second_ref[...] = low(second)
        scaled_ref[...] = scaled
        inverse_ref[...] = inverse

    outs = [
        shape((slots, features), LOW), shape((slots, features), F32), shape((slots, features), LOW),
        shape((slots, features), F32), shape((slots, 1), F32),
    ]
    flops = 2 * slots * features * features
    return call(kernel, outs, [base], [weight, source, gain[None]] + list(pieces), flops=flops)


def own_slab(attention_in, extra, base, below):
    rows, triple = attention_in.shape
    columns = triple // (3 * lax.axis_size("narrow"))
    below_rows = below.shape[0] if below is not None else 0
    wide_extra = extra.shape[1] if extra is not None else 0

    def kernel(base_ref, weight_ref, *refs):
        refs, out = list(refs[:-1]), refs[-1]
        for part in range(3):
            start = pl.multiple_of(part * (triple // 3) + base_ref[0] * columns, columns)
            out[:rows, part * columns : (part + 1) * columns] = weight_ref[:, pl.ds(start, columns)]
        if extra is not None:
            out[:rows, 3 * columns :] = refs.pop(0)[...]
        if below is not None:
            out[rows:, :] = jnp.zeros((below_rows, 3 * columns + wide_extra), LOW)
            out[rows:, : below.shape[1]] = refs.pop(0)[...]

    arrays = [attention_in] + [a for a in (extra, below) if a is not None]
    outs = [shape((rows + below_rows, 3 * columns + wide_extra), LOW)]
    return call(kernel, outs, [base], arrays)[0]


def join_slab(found, rows, parts, at_wide, below=0):
    across, beside = found
    pieces = [p for pair in zip(across, beside) for p in pair]
    count = len(pieces)

    def kernel(base_ref, *refs):
        for k in range(count):
            start = pl.multiple_of((base_ref[0] ^ k) * rows, rows)
            at = 0
            for i, columns in enumerate(parts):
                refs[count + i][pl.ds(start, rows), :] = refs[k][:rows, at : at + columns]
                at += columns
            if below:
                start = pl.multiple_of((base_ref[0] ^ k) * below, below)
                refs[-1][pl.ds(start, below), :] = refs[k][rows:, :rows]

    outs = [shape((count * rows, columns), LOW) for columns in parts]
    if below:
        outs.append(shape((count * below, rows), LOW))
    return call(kernel, outs, [at_wide], pieces)


def spread_columns(pieces, base):
    count, (rows, triple) = len(pieces), pieces[0].shape
    columns = triple // 3

    def kernel(base_ref, *refs):
        for k in range(count):
            for part in range(3):
                start = part * count * columns + (base_ref[0] ^ k) * columns
                refs[count][:, pl.ds(pl.multiple_of(start, columns), columns)] = refs[k][
                    :, part * columns : (part + 1) * columns
                ].astype(F32)

    return call(kernel, [shape((rows, count * triple), F32)], [base], pieces)[0]


def reorder(whole, slots, at_wide, outward):
    count = whole.shape[0] // slots
    order = list(range(0, count, 2)) + list(range(1, count, 2))

    def kernel(base_ref, whole_ref, out_ref):
        for i, k in enumerate(order):
            start = pl.multiple_of((base_ref[0] ^ k) * slots, slots)
            if outward:
                out_ref[pl.ds(start, slots), :] = whole_ref[i * slots : (i + 1) * slots, :]
            else:
                out_ref[i * slots : (i + 1) * slots, :] = whole_ref[pl.ds(start, slots), :]

    return call(kernel, [shape(whole.shape, whole.dtype)], [at_wide], [whole])[0]


def outer_pair(pieces, grad_packed, context, grad_attended):
    count, (slots, features) = len(pieces), pieces[0].shape
    columns = grad_packed.shape[1]

    def kernel(*refs):
        left = jnp.concatenate([r[...] for r in refs[:count]], axis=0)
        packed_ref, context_ref, attended_ref, out = refs[count:]
        out[:, :columns] = low(product(left, packed_ref[...], 0, 0))
        out[:, columns:] = low(product(context_ref[...], attended_ref[...], 0, 0))

    outs = [shape((features, columns + context.shape[1]), LOW)]
    flops = 2 * slots * features * (count * columns + context.shape[1])
    arrays = list(pieces) + [grad_packed, context, grad_attended]
    return call(kernel, outs, [], arrays, flops=flops)[0]


def stack_own(dense, pair, columns):
    units, features = dense.shape
    rows = pair.shape[0]

    def kernel(dense_ref, pair_ref, out_ref):
        out_ref[:units, :] = dense_ref[...]
        out_ref[units : units + rows, :] = pair_ref[:, columns:]
        out_ref[units + rows :, columns:] = jnp.zeros((rows, features - columns), LOW)
        out_ref[units + rows :, :columns] = pair_ref[:, :columns]

    return call(kernel, [shape((units + 2 * rows, features), LOW)], [], [dense, pair])[0]


def split_gathered(gathered, rows, columns):
    narrow = lax.axis_size("narrow")
    features = gathered.shape[1]
    block = gathered.shape[0] // narrow
    units = block - 2 * rows
    half = units * narrow // 2
    fold = features // half
    third = columns // 3

    def kernel(whole_ref, up_ref, down_ref, in_ref, out_ref):
        total = None
        for j in range(narrow):
            own = whole_ref[j * block : j * block + units, :].astype(F32)
            if j < narrow // 2:
                for i in range(fold):
                    at = i * half + j * units
                    up_ref[at : at + units, :] = own[:, i * half : (i + 1) * half]
            else:
                at = (j - narrow // 2) * units
                down_ref[at : at + units, :] = own
            at = j * block + units
            found = whole_ref[at : at + rows, :].astype(F32)
            total = found if total is None else total + found
            at += rows
            for part in range(3):
                start = part * narrow * third + j * third
                in_ref[:, start : start + third] = whole_ref[
                    at : at + rows, part * third : (part + 1) * third
                ].astype(F32)
        out_ref[...] = total

    outs = [
        shape((features, half), F32), shape((half, features), F32),
        shape((rows, narrow * columns), F32), shape((rows, features), F32),
    ]
    return call(kernel, outs, [], [gathered])


def dense_products(parts):
    return low(up_product(parts)), low(down_product(parts))


def dense_join(parts):
    up, down = parts
    features, units = up.shape
    fold = features // units

    def kernel(up_ref, down_ref, out_ref):
        for i in range(fold):
            out_ref[:units, i * units : (i + 1) * units] = up_ref[i * units : (i + 1) * units, :]
        out_ref[units:, :] = down_ref[...]

    return call(kernel, [shape((2 * units, features), LOW)], [], [up, down])[0]


def narrow_scatter(whole):
    return lax.psum_scatter(whole, "narrow", scatter_dimension=0, tiled=True)


def narrow_gather(own):
    return lax.all_gather(own, "narrow", axis=0, tiled=True)


def dense_outputs(gathered):
    units, features = gathered.shape[0] // 2, gathered.shape[1]
    fold = features // units

    def kernel(whole_ref, up_ref, down_ref):
        for i in range(fold):
            up_ref[i * units : (i + 1) * units, :] = whole_ref[
                :units, i * units : (i + 1) * units
            ].astype(F32)
        down_ref[...] = whole_ref[units:, :].astype(F32)

    return call(kernel, [shape((features, units), F32), shape((units, features), F32)], [], [gathered])


def gather_wide(own):
    return lax.all_gather(own, "wide", axis=0, tiled=True)


def after(value, *others):
    return lax.optimization_barrier((value,) + others)[0]


def reversed_order(count):
    bits = count.bit_length() - 1
    return [sum((i >> b & 1) << (bits - 1 - b) for b in range(bits)) for i in range(count)]


def outer_halves(lefts, right, base):
    count = len(lefts)
    wide = lax.axis_size("wide")
    slots, features = lefts[0].shape
    columns = right.shape[1]
    rows = features // wide
    order = reversed_order(wide)

    def kernel(base_ref, *refs):
        right_ref, keep_ref, send_ref, total_ref = refs[count:]
        left = refs[0][...] if count == 1 else jnp.concatenate([r[...] for r in refs[:count]], axis=0)
        total_ref[...] = product(left, right_ref[...], 0, 0)
        for i, k in enumerate(order):
            start = pl.multiple_of((base_ref[0] ^ k) * rows, rows)
            out, at = (keep_ref, i) if i < wide // 2 else (send_ref, i - wide // 2)
            out[at * rows : (at + 1) * rows, :] = low(total_ref[pl.ds(start, rows), :])

    outs = [shape((features // 2, columns), LOW)] * 2
    scratch = [pltpu.VMEM((features, columns), F32)]
    flops = 2 * count * slots * features * columns
    return call(kernel, outs, [base], list(lefts) + [right], scratch, flops)


def pair_sum(own, received, slots):
    count = own.shape[0] // slots
    features = own.shape[1]

    def kernel(own_ref, received_ref, *outs):
        for k in range(count):
            at = slice(k * slots, (k + 1) * slots)
            total = own_ref[at, :] + received_ref[at, :].astype(F32)
            outs[k][...] = total if k == 0 else low(total)

    outs = [shape((slots, features), F32)] + [shape((slots, features), LOW)] * (count - 1)
    return call(kernel, outs, [], [own, received])


def halving_step(halves, distance):
    keep, send = halves
    total = keep.astype(F32) + swap(send, "wide", distance).astype(F32)
    if 2 * distance == lax.axis_size("wide"):
        return total
    half = total.shape[0] // 2
    return total[:half], low(total[half:])


def halving_rest(halves, distance):
    while distance < lax.axis_size("wide"):
        halves = halving_step(halves, distance)
        distance *= 2
    return halves


def together(value, other):
    return lax.optimization_barrier((value, other))


def narrow_sum(value, first):
    narrow = lax.axis_size("narrow")
    bits = narrow.bit_length() - 1
    for b in range(bits):
        value = value + swap(low(value), "narrow", 1 << (b + first) % bits).astype(F32)
    return value


def narrow_rest(value):
    distance = 2
    while distance < lax.axis_size("narrow"):
        value = value + swap(low(value), "narrow", distance).astype(F32)
        distance *= 2
    return value


def axis_sum(value, axis, distance=1):
    while distance < lax.axis_size(axis):
        value = value + swap(value, axis, distance)
        distance *= 2
    return value


def layer_norm(source, gain):
    centre = source - jnp.mean(source, axis=-1, keepdims=True)
    inverse = lax.rsqrt(jnp.mean(centre * centre, axis=-1, keepdims=True) + 1e-05)
    scaled = centre * inverse
    return scaled * gain, scaled, inverse


def norm_back(upstream, scaled, inverse, gain):
    grad_scaled = upstream * gain
    mean_first = jnp.mean(grad_scaled, axis=-1, keepdims=True)
    mean_second = jnp.mean(grad_scaled * scaled, axis=-1, keepdims=True)
    return (
        inverse * (grad_scaled - mean_first - scaled * mean_second),
        jnp.sum(upstream * scaled, axis=0),
    )


def activate(source):
    return jax.nn.gelu(source)


def activation_back(source, upstream):
    return jax.vjp(activate, source)[1](upstream)[0]


def masked_scores(queries, keys, allowed):
    scores = product(queries, keys, 1, 1) * HEAD_DIM ** (-0.5)
    return jnp.where(allowed, scores, -1e30)


def allowed_of(length, slots):
    rows_at = lax.broadcasted_iota(jnp.int32, (slots, slots), 0)
    cols_at = lax.broadcasted_iota(jnp.int32, (slots, slots), 1)
    return (cols_at <= rows_at) & (cols_at < length)


def head_parts(packed, head, columns):
    return [
        packed[:, part * columns + head * HEAD_DIM : part * columns + (head + 1) * HEAD_DIM]
        for part in range(3)
    ]


def attention(pieces, gain, weight, lengths):
    count, (slots, features) = len(pieces), pieces[0].shape
    columns = weight.shape[1] // 3
    raw = gain is not None

    def kernel(lengths_ref, *refs):
        ins, weight_ref, refs = refs[:count], refs[count], refs[count + 1 :]
        if raw:
            gain_ref, refs = refs[0], refs[1:]
        packed_ref, level_ref, outs = refs[0], refs[1], refs[2 : count + 2]
        levels = []
        for j in range(count):
            if raw:
                rows = low(layer_norm(ins[j][...].astype(F32), gain_ref[...])[0])
                refs[count + 2 + j][...] = rows
            else:
                rows = ins[j][...]
            packed = low(product(rows, weight_ref[...], 1, 0))
            packed_ref[j] = packed
            allowed = allowed_of(lengths_ref[j], slots)
            found = []
            for head in range(columns // HEAD_DIM):
                queries, keys, values = head_parts(packed, head, columns)
                scores = masked_scores(queries, keys, allowed)
                top = jnp.max(scores, axis=-1, keepdims=True)
                raised = jnp.exp(scores - top)
                weight_sum = jnp.sum(raised, axis=-1, keepdims=True)
                levels.append(top + jnp.log(weight_sum))
                found.append(product(low(raised / weight_sum), values, 1, 0))
            outs[j][...] = low(jnp.concatenate(found, axis=1))
        level_ref[...] = jnp.concatenate(levels, axis=1)

    outs = [shape((count, slots, 3 * columns), LOW)]
    outs += [shape((slots, count * columns // HEAD_DIM), F32)]
    outs += [shape((slots, columns), LOW)] * count
    arrays = list(pieces) + [weight]
    if raw:
        outs += [shape((slots, features), LOW)] * count
        arrays.append(gain[None])
    flops = 2 * count * slots * features * 3 * columns
    packed, levels, *found = call(kernel, outs, [lengths], arrays, flops=flops)
    return (packed, levels), found[:count], found[count:] if raw else pieces


def attention_back(packed, grads, lengths):
    packed, levels = packed
    count, (slots, columns) = len(grads), grads[0].shape
    scaling = HEAD_DIM ** (-0.5)

    def kernel(lengths_ref, packed_ref, level_ref, *refs):
        out = refs[count]
        for j in range(count):
            allowed = allowed_of(lengths_ref[j], slots)
            whole = packed_ref[j]
            grad_whole = refs[j][...]
            found = [[], [], []]
            for head in range(columns // HEAD_DIM):
                queries, keys, values = head_parts(whole, head, columns)
                grad_head = grad_whole[:, head * HEAD_DIM : (head + 1) * HEAD_DIM]
                at = j * (columns // HEAD_DIM) + head
                scores = masked_scores(queries, keys, allowed)
                softened = jnp.exp(scores - level_ref[:, at : at + 1])
                grad_soft = product(grad_head, values, 1, 1)
                inner = jnp.sum(softened * grad_soft, axis=-1, keepdims=True)
                grad_scores = low(softened * (grad_soft - inner))
                found[0].append(scaling * product(grad_scores, keys, 1, 0))
                found[1].append(scaling * product(grad_scores, queries, 0, 0))
                found[2].append(product(low(softened), grad_head, 0, 0))
            out[j * slots : (j + 1) * slots, :] = low(
                jnp.concatenate(found[0] + found[1] + found[2], axis=1)
            )

    outs = [shape((count * slots, 3 * columns), LOW)]
    return call(kernel, outs, [lengths], [packed, levels] + list(grads))[0]


def normed_back(grad_packed, weight, count):
    slots, features = grad_packed.shape[0] // count, weight.shape[0]

    def kernel(grad_ref, weight_ref, *outs):
        whole = low(product(grad_ref[...], weight_ref[...], 1, 1))
        for j in range(count):
            outs[j][...] = whole[j * slots : (j + 1) * slots]

    outs = [shape((slots, features), LOW)] * count
    flops = 2 * count * slots * features * weight.shape[1]
    return call(kernel, outs, [], [grad_packed, weight], flops=flops)


def wide_across(own):
    return [own] + [swap(own, "wide", apart) for apart in range(2, lax.axis_size("wide"), 2)]


def wide_pieces(own):
    across = wide_across(own)
    return across, [swap(piece, "wide", 1) for piece in across]


def wide_join(pieces):
    across, beside = pieces
    return join_rows(list(across) + list(beside))


def wide_sends(own, received, slots):
    parts = pair_sum(own, received, slots)
    return [parts[0]] + [swap(p, "wide", 2 * (i + 1)) for i, p in enumerate(parts[1:])]


def wide_total(parts):
    total = parts[0]
    for part in parts[1:]:
        total = total + part.astype(F32)
    return total


def wide_sums(halves, slots):
    own, other = halves
    return wide_total(wide_sends(own, swap(other, "wide", 1), slots))


def place(labels, experts, capacity):
    blocks, slots = labels.shape
    first = jnp.arange(blocks, dtype=jnp.int32)[:, None] * capacity - 1
    places = jnp.arange(blocks * capacity, dtype=jnp.int32)
    selects = []
    for expert in experts:
        chosen = labels == expert
        at = jnp.where(chosen, first + jnp.cumsum(chosen.astype(jnp.int32), axis=1), -1)
        selects.append(low(places[:, None] == at.reshape(-1)[None, :]))
    return selects


def picked(selects, rows):
    return [low(product(select, rows, 1, 0)) for select in selects]


def exchanged(sent, slices):
    narrow = lax.axis_size("narrow")
    return join_rows(
        [sent[j // slices] if j == 0 else swap(sent[j // slices], "narrow", j) for j in range(narrow)]
    )


def to_experts(selects, rows, slices):
    return exchanged(picked(selects, rows), slices)


def from_experts(selects, outcome, slices):
    narrow = lax.axis_size("narrow")
    parts = outcome.reshape(narrow, -1, outcome.shape[-1])
    found = []
    for r in range(len(selects)):
        total = None
        for j in range(r * slices, (r + 1) * slices):
            part = parts[j] if j == 0 else swap(low(parts[j]), "narrow", j).astype(F32)
            total = part if total is None else total + part
        found.append(low(total))
    return found


def spread_of(selects, found, at):
    total = None
    for select, rows in zip(selects, found):
        part = product(select[:, at], rows, 0, 0)
        total = part if total is None else total + part
    return total


def layer_forward(source, raw, weights, selects, lengths, at_narrow, slices, second_work=None, third_work=None):
    norm_first, attention_in, attention_out, norm_second, mixer, up, down, expert_up, expert_down = weights
    slots, features = source.shape
    wide, narrow = lax.axis_size("wide"), lax.axis_size("narrow")
    normed, scaled_one, inverse_one = layer_norm(source, norm_first)
    own = low(normed)
    pieces = raw
    if raw is None:
        pieces = [own] + [swap(own, "narrow", j) for j in range(1, narrow)]
    packed, contexts, pieces = attention(
        pieces, None if raw is None else norm_first, attention_in, lengths
    )
    context, middle, second, scaled_two, inverse_two = attended(
        [contexts[0]] + [swap(contexts[j], "narrow", j) for j in range(1, narrow)],
        attention_out, source, norm_second, at_narrow,
    )
    across, beside = wide_pieces(second)
    if second_work is not None:
        across, second_found = together(across, second_work(second))
    rows = wide_join((across, beside))
    mixing = jax.nn.softmax(jnp.dot(rows, mixer, preferred_element_type=F32), axis=-1)
    pre = jnp.dot(rows, up, preferred_element_type=F32)
    act = low(activate(pre))
    third_found = None if third_work is None else third_work(rows, second_found)
    expert_rows, (mixing, pre, act, third_found) = together(
        to_experts(selects, rows, slices), (mixing, pre, act, third_found)
    )
    expert_pre = jnp.dot(expert_rows, expert_up, preferred_element_type=F32)
    expert_act = low(activate(expert_pre))
    kept = (
        scaled_one, inverse_one, pieces, packed, context, scaled_two, inverse_two,
        (rows, mixing, expert_rows, expert_pre, expert_act, pre, act),
    )
    return (middle, kept) if second_work is None else (middle, kept, third_found)


def experts_found(kept, weights, selects, slices, gate=None):
    act = kept[7][4] if gate is None else after(kept[7][4], gate)
    outcome = jnp.dot(act, weights[8], preferred_element_type=F32)
    return from_experts(selects, outcome, slices)


def merged_halves(kept, weights, selects, found, slots):
    mixing, act = kept[7][1], kept[7][6]

    def merged(at):
        dense = jnp.dot(act[at], weights[6], preferred_element_type=F32)
        return mixing[at, :1] * dense + mixing[at, 1:] * spread_of(selects, found, at)

    half = act.shape[0] // 2
    return merged(slice(0, half)), low(merged(slice(half, 2 * half)))


def dense_back_of(through, kept, weights):
    rows, mixing, _, _, _, pre, act = kept[7]
    dense_dot = jnp.sum(act.astype(F32) * through, axis=1, keepdims=True)
    dense_logit = mixing[:, :1] * mixing[:, 1:] * dense_dot
    grad_pre = low(activation_back(pre, mixing[:, :1] * through))
    return grad_pre, dense_logit


def experts_back(upstream, gathered, kept, weights, selects, slices, beneath, alongside):
    norm_second, mixer, up, down, expert_up, expert_down = weights[3:]
    scaled_two, inverse_two = kept[5:7]
    rows, mixing, expert_rows, expert_pre, expert_act, pre, act = kept[7]
    slots = upstream.shape[0]
    wide = lax.axis_size("wide")
    mixer_gap = (mixer[:, 0].astype(F32) - mixer[:, 1].astype(F32))[None]
    grads, expert_grads, through, dense_back = gathered
    expert_mixing = jax.nn.softmax(
        jnp.dot(expert_rows, mixer, preferred_element_type=F32), axis=-1
    )
    expert_dot = jnp.sum(expert_act.astype(F32) * through, axis=1, keepdims=True)
    expert_logit = -expert_mixing[:, :1] * expert_mixing[:, 1:] * expert_dot
    expert_grad_pre = low(activation_back(expert_pre, expert_mixing[:, 1:] * through))
    expert_back = product(expert_grad_pre, expert_up, 1, 1) + expert_logit * mixer_gap
    if callable(dense_back):
        dense_back = dense_back(expert_back)
    grad_pre, dense_logit = dense_back
    dense = (rows, grad_pre, act, mixing[:, :1], grads)
    found = from_experts(selects, expert_back, slices)
    experts = (
        expert_rows, expert_grad_pre,
        expert_act, expert_mixing[:, 1:], expert_grads,
    )
    found, beneath_found = together(found, beneath(expert_back, experts, dense))

    def merged(at):
        dense_back = product(grad_pre[at], up, 1, 1) + dense_logit[at] * mixer_gap
        return dense_back + spread_of(selects, found, at)

    half = grad_pre.shape[0] // 2
    halves = merged(slice(0, half)), low(merged(slice(half, 2 * half)))
    parts = wide_sends(halves[0], swap(halves[1], "wide", 1), slots)
    rows, dense_logit, expert_rows, expert_logit = after(
        (rows, dense_logit, expert_rows, expert_logit), parts[0]
    )
    grad_gap = jnp.sum(rows.astype(F32) * dense_logit, axis=0) + jnp.sum(
        expert_rows.astype(F32) * expert_logit, axis=0
    )
    grad_second, (grad_gap, alongside_found) = together(
        wide_total(parts), (grad_gap, alongside(parts[0], halves[1], beneath_found, experts, dense))
    )
    grad_norm_part, grad_norm_second = norm_back(grad_second, scaled_two, inverse_two, norm_second)
    return (
        upstream + grad_norm_part, dense, experts, (grad_norm_second, grad_gap),
        beneath_found, alongside_found,
    )


def up_product(parts):
    return product(parts[0], parts[1], 0, 0)


def down_product(parts):
    act, mix, grads = parts[2:]
    return product(act, low(mix * grads.astype(F32)), 0, 0)


def attention_grads(grad_middle, kept, weights, lengths, at_narrow, hold, filler):
    norm_first, attention_in, attention_out = weights[:3]
    scaled_one, inverse_one, pieces, packed, context = kept[:5]
    narrow = lax.axis_size("narrow")
    grad_attended = low(grad_middle)
    grad_contexts = context_back(grad_attended, attention_out, narrow, at_narrow)
    grad_contexts = [grad_contexts[0]] + [
        swap(grad_contexts[j], "narrow", j) for j in range(1, narrow)
    ]
    grad_packed = attention_back(packed, grad_contexts, lengths)
    grad_packed, hold = together(grad_packed, hold)
    parts = normed_back(grad_packed, attention_in, narrow)
    weight_grads = (pieces, after(grad_packed, parts), context, grad_attended)
    filled = filler(parts[0])
    parts = [parts[0]] + [swap(parts[j], "narrow", j) for j in range(1, narrow)]
    parts, filled = together(parts, filled)
    grad_normed = sum(part.astype(F32) for part in parts)
    grad_norm_part, grad_norm_first = norm_back(grad_normed, scaled_one, inverse_one, norm_first)
    return grad_middle + grad_norm_part, grad_norm_first, weight_grads, hold, filled


def last_grads(
    grad_middle, kept, weights, lengths, at_narrow, at_wide, dense, pair, narrow_columns, early
):
    norm_first, attention_in, attention_out = weights[:3]
    scaled_one, inverse_one, pieces, packed, context = kept[:5]
    narrow = lax.axis_size("narrow")
    grad_attended = low(grad_middle)
    grad_contexts = context_back(grad_attended, attention_out, narrow, at_narrow)
    grad_contexts = [grad_contexts[0]] + [
        swap(grad_contexts[j], "narrow", j) for j in range(1, narrow)
    ]
    out_halves = outer_halves([context], after(grad_attended, grad_contexts[-1]), at_wide)
    grad_contexts, out_halves = together(grad_contexts, halving_step(out_halves, 1))
    rows = pair.shape[0]
    gathered = narrow_gather(stack_own(dense, after(pair, grad_contexts), narrow_columns))
    out_halves = halving_step(out_halves, 2)
    early = after(early, grad_contexts)
    early = early + swap(early, "narrow", 1)
    grad_packed = attention_back(packed, grad_contexts, lengths)
    grad_packed, (out_halves, early) = together(grad_packed, (out_halves, early))
    in_halves = outer_halves(pieces, grad_packed, at_wide)
    in_halves, early = together(in_halves, axis_sum(early, "narrow", 2))
    parts = normed_back(after(grad_packed, in_halves), attention_in, narrow)
    in_halves = halving_step(halving_step(in_halves, 1), 2)
    parts = [parts[0]] + [swap(parts[j], "narrow", j) for j in range(1, narrow)]
    parts = after(parts, in_halves)
    grad_normed = sum(part.astype(F32) for part in parts)
    grad_norm_part, grad_norm_first = norm_back(grad_normed, scaled_one, inverse_one, norm_first)
    grad_inputs = grad_middle + grad_norm_part
    out_sum = halving_rest(out_halves, 4)
    in_sum, (first, grad_inputs) = together(
        low(halving_rest(in_halves, 4)), (grad_norm_first[None], grad_inputs)
    )
    out_sum = after(out_sum, in_halves)
    out_sum = out_sum + swap(low(out_sum), "narrow", 1).astype(F32)
    in_pieces = [in_sum] + [swap(in_sum, "narrow", j) for j in range(1, narrow)]
    in_pieces, gathered = together(
        in_pieces, split_gathered(after(gathered, in_sum), rows, narrow_columns)
    )
    vectors = axis_sum(jnp.concatenate([axis_sum(first, "narrow"), early], axis=0), "wide")
    out_sum = narrow_rest(after(out_sum, in_sum))
    return (
        grad_inputs, (spread_columns(in_pieces, at_narrow), out_sum), vectors, gathered
    )


def body(
    inputs, cotangent, seq_len, shallow_routes, deep_routes,
    shallow_norm_first, shallow_attention_in, shallow_attention_out, shallow_norm_second,
    shallow_dense_up, shallow_dense_down, shallow_mixer, shallow_expert_up, shallow_expert_down,
    deep_norm_first, deep_attention_in, deep_attention_out, deep_norm_second,
    deep_dense_up, deep_dense_down, deep_mixer, deep_expert_up, deep_expert_down,
):
    wide, narrow = lax.axis_size("wide"), lax.axis_size("narrow")
    wide_at, narrow_at = lax.axis_index("wide"), lax.axis_index("narrow")
    at_wide, at_narrow = wide_at.reshape(1), narrow_at.reshape(1)
    slots, features = inputs.shape
    small = jnp.stack(
        [
            shallow_norm_first, shallow_norm_second, deep_norm_first, deep_norm_second,
            shallow_mixer[:, 0], shallow_mixer[:, 1], deep_mixer[:, 0], deep_mixer[:, 1],
        ]
    )
    narrow_columns = 3 * features // narrow
    rows_own = shallow_attention_in.shape[0]
    input_pieces = [inputs] + [swap(inputs, "narrow", j) for j in range(1, narrow)]
    across = wide_across(own_slab(shallow_attention_in, None, at_narrow, small))
    lengths = seq_len[wide_at * narrow + (narrow_at ^ jnp.arange(narrow))]
    deep_slab = own_slab(deep_attention_in, None, at_narrow, None)
    across, (input_pieces, lengths, deep_slab) = together(
        across, (input_pieces, lengths, deep_slab)
    )
    in_pieces = across, [swap(piece, "wide", 1) for piece in across]
    shallow_in, small = join_slab(
        in_pieces, rows_own, [narrow_columns], at_wide, small.shape[0]
    )
    shallow_out = gather_wide(after(shallow_attention_out, in_pieces[0][-1]))
    small = jnp.transpose(small.reshape(wide, 8, -1), (1, 0, 2)).reshape(8, features)
    gains = small[:4].astype(F32)
    def selects_of(routes, slices):
        table = routes.reshape(wide, narrow, slots)
        own = lax.dynamic_index_in_dim(table, narrow_at, axis=1, keepdims=False)
        capacity = slices * max(1, 3 * slots // (2 * wide * narrow))
        groups = narrow // slices
        experts = [wide_at * groups + ((narrow_at // slices) ^ r) for r in range(groups)]
        order = jnp.array(list(range(0, wide, 2)) + list(range(1, wide, 2)))
        return place(own[wide_at ^ order], experts, capacity)

    shallow_selects = selects_of(shallow_routes, SLICES_SHALLOW)
    deep_selects = selects_of(deep_routes, SLICES_DEEP)
    shallow = (
        gains[0], shallow_in, shallow_out, gains[1], small[4:6].T,
        shallow_dense_up, shallow_dense_down, shallow_expert_up[0], shallow_expert_down[0],
    )
    middle, kept_shallow = layer_forward(
        inputs.astype(F32), input_pieces, shallow, shallow_selects, lengths, at_narrow, SLICES_SHALLOW
    )
    deep_in = gather_wide(after(deep_slab, kept_shallow[7][0]))
    deep_out = gather_wide(after(deep_attention_out, kept_shallow[7][2]))
    found = experts_found(kept_shallow, shallow, shallow_selects, SLICES_SHALLOW)
    halves = merged_halves(kept_shallow, shallow, shallow_selects, found, slots)
    total = wide_sums(halves, slots)
    passed = middle + total
    all_grads = gather_wide(after(cotangent, total))
    deep = (
        gains[2], deep_in, deep_out, gains[3], small[6:8].T,
        deep_dense_up, deep_dense_down, deep_expert_up[0], deep_expert_down[0],
    )
    def second_work(second):
        grads = reorder(after(all_grads, second), slots, at_wide, False)
        expert_grads = to_experts(deep_selects, grads, SLICES_DEEP)
        return grads, expert_grads, product(grads, deep_dense_down, 1, 1)

    def third_work(rows, found):
        grads, expert_grads, through = found
        return grads, expert_grads, through, product(after(expert_grads, rows), deep_expert_down[0], 1, 1)

    middle, kept_deep, gathered = layer_forward(
        passed, None, deep, deep_selects, lengths, at_narrow, SLICES_DEEP, second_work, third_work
    )
    def deep_result(found):
        halves = merged_halves(kept_deep, deep, deep_selects, found, slots)
        return reorder(
            jnp.concatenate([low(halves[0]), halves[1]], axis=0), slots, at_wide, True
        )

    grad_middle, _, deep_experts, deep_rows, (whole, found), result = experts_back(
        cotangent.astype(F32),
        gathered[:2] + (
            gathered[3],
            lambda token: dense_back_of(after(gathered[2], token), kept_deep, deep),
        ), kept_deep,
        deep, deep_selects, SLICES_DEEP,
        lambda token, experts, dense: (
            dense_join(dense_products(after(dense, token))),
            experts_found(kept_deep, deep, deep_selects, SLICES_DEEP, token),
        ),
        lambda token, other, found, experts, dense: deep_result(after(found[1], token)),
    )
    total = lax.psum_scatter(result, "wide", scatter_dimension=0, tiled=True)
    grad_passed, deep_first, outer_parts, whole, deep_down = attention_grads(
        grad_middle, kept_deep, deep, lengths, at_narrow, narrow_scatter(whole),
        lambda token: down_product(after(deep_experts, token)),
    )
    passed_low = low(grad_passed)
    across, beside = wide_pieces(passed_low)
    across, total = together(across, total)
    grads = wide_join((across, beside))
    pair = outer_pair(*after(outer_parts, grads))
    expert_grads, (pair, dense_back) = together(
        to_experts(shallow_selects, grads, SLICES_SHALLOW),
        (
            pair,
            dense_back_of(product(grads, shallow_dense_down, 1, 1), kept_shallow, shallow),
        ),
    )
    pair = lax.psum_scatter(pair, "wide", scatter_dimension=0, tiled=True)
    whole = narrow_gather(after(whole, passed_low))
    grad_middle, _, _, shallow_rows, (joined, deep_up), (shallow_experts, pair, deep_dense) = experts_back(
        grad_passed,
        (grads, expert_grads, product(expert_grads, shallow_expert_down[0], 1, 1), dense_back),
        kept_shallow, shallow, shallow_selects, SLICES_SHALLOW,
        lambda token, experts, dense: (
            dense_join(dense_products(after(dense, token))),
            up_product(after(deep_experts, token)),
        ),
        lambda token, other, found, experts, dense: (
            [f(after(experts, token)) for f in (up_product, down_product)], pair,
            dense_outputs(after(whole, token)),
        ),
    )
    shallow_up, shallow_down = shallow_experts
    early = jnp.stack(list(shallow_rows) + [deep_first] + list(deep_rows))
    grad_inputs, (grad_shallow_in, grad_shallow_out), vectors, gathered = last_grads(
        grad_middle, kept_shallow, shallow, lengths, at_narrow, at_wide,
        narrow_scatter(joined), pair, narrow_columns, early,
    )
    *shallow_dense, grad_deep_in, grad_deep_out = gathered
    output = middle + total.astype(F32)
    deep_up, deep_down = deep_up[None], deep_down[None]
    shallow_up, shallow_down = shallow_up[None], shallow_down[None]
    grads_shallow = (
        grad_shallow_in, grad_shallow_out, *shallow_dense, shallow_up, shallow_down,
    )
    grads_deep = (
        grad_deep_in, grad_deep_out, *deep_dense, deep_up, deep_down,
    )
    vectors = lax.dynamic_slice_in_dim(vectors, wide_at * (features // wide), features // wide, axis=1)

    def outputs_of(grads, rows):
        grad_mixer = jnp.stack([rows[2], -rows[2]], axis=1)
        return (
            rows[0], grads[0], grads[1], rows[1], grads[2], grads[3], grad_mixer, grads[4], grads[5],
        )

    return (
        (low(output), grad_inputs)
        + outputs_of(grads_shallow, vectors[:3])
        + outputs_of(grads_deep, vectors[3:])
    )


def solution(mesh):
    both = ("wide", "narrow")
    parameters = (
        P("wide"), P("wide", None), P("wide", None), P("wide"), P(None, "wide"),
        P("wide", None), P("wide", None), P(both, None, None), P(both, None, None),
    )
    return jax.shard_map(
        body,
        mesh=mesh,
        in_specs=(P(both, None), P(both, None), P(), P(), P()) + parameters + parameters,
        out_specs=(P(both, None), P(both, None)) + parameters + parameters,
        check_vma=False,
    )
```

```python
import jax
import jax.numpy as jnp
from jax import lax
from jax.experimental import pallas as pl
from jax.experimental.pallas import tpu as pltpu
from jax.sharding import PartitionSpec as P

HEAD_DIM = 64
SLICES_SHALLOW = 4
SLICES_DEEP = 2
F32 = jnp.float32
LOW = jnp.bfloat16
VMEM_LIMIT = 60 * 1024 * 1024


def low(value):
    return value.astype(LOW)


def swap(array, axis, distance):
    return lax.ppermute(array, axis, [(i, i ^ distance) for i in range(lax.axis_size(axis))])


def product(left, right, left_dim, right_dim):
    return lax.dot_general(
        left, right, (((left_dim,), (right_dim,)), ((), ())), preferred_element_type=F32
    )


def vmem():
    return pl.BlockSpec(memory_space=pltpu.VMEM)


def smem():
    return pl.BlockSpec(memory_space=pltpu.SMEM)


def call(kernel, outs, scalars, arrays, scratch=(), flops=0):
    moved = sum(a.size * a.dtype.itemsize for a in list(arrays) + list(outs))
    return pl.pallas_call(
        kernel,
        out_shape=tuple(outs),
        in_specs=[smem()] * len(scalars) + [vmem()] * len(arrays),
        out_specs=tuple(vmem() for _ in outs),
        scratch_shapes=list(scratch),
        compiler_params=pltpu.CompilerParams(vmem_limit_bytes=VMEM_LIMIT),
        cost_estimate=pl.CostEstimate(flops=flops, bytes_accessed=moved, transcendentals=0),
    )(*scalars, *arrays)


def shape(dims, kind):
    return jax.ShapeDtypeStruct(dims, kind)


def join_rows(pieces):
    if len(pieces) == 1:
        return pieces[0]
    count, (rows, columns) = len(pieces), pieces[0].shape

    def kernel(*refs):
        for k in range(count):
            refs[count][k * rows : (k + 1) * rows, :] = refs[k][...]

    return call(kernel, [shape((count * rows, columns), pieces[0].dtype)], [], pieces)[0]


def context_back(grads, weight, count, base):
    slots, features = grads.shape
    columns = features // count

    def kernel(base_ref, grads_ref, weight_ref, *outs):
        for k in range(count):
            start = pl.multiple_of((base_ref[0] ^ k) * columns, columns)
            outs[k][...] = low(product(grads_ref[...], weight_ref[pl.ds(start, columns), :], 1, 1))

    outs = [shape((slots, columns), LOW)] * count
    flops = 2 * slots * features * features
    return call(kernel, outs, [base], [grads, weight], flops=flops)


def attended(pieces, weight, source, gain, base):
    count, (slots, columns) = len(pieces), pieces[0].shape
    features = source.shape[1]

    def kernel(base_ref, weight_ref, source_ref, gain_ref, *refs):
        context_ref, middle_ref, second_ref, scaled_ref, inverse_ref = refs[count:]
        total = source_ref[...]
        for k in range(count):
            start = pl.multiple_of((base_ref[0] ^ k) * columns, columns)
            context_ref[:, pl.ds(start, columns)] = refs[k][...]
            total = total + product(refs[k][...], weight_ref[pl.ds(start, columns), :], 1, 0)
        middle_ref[...] = total
        second, scaled, inverse = layer_norm(total, gain_ref[...])
        second_ref[...] = low(second)
        scaled_ref[...] = scaled
        inverse_ref[...] = inverse

    outs = [
        shape((slots, features), LOW), shape((slots, features), F32), shape((slots, features), LOW),
        shape((slots, features), F32), shape((slots, 1), F32),
    ]
    flops = 2 * slots * features * features
    return call(kernel, outs, [base], [weight, source, gain[None]] + list(pieces), flops=flops)


def own_slab(attention_in, extra, base, below):
    rows, triple = attention_in.shape
    columns = triple // (3 * lax.axis_size("narrow"))
    below_rows = below.shape[0] if below is not None else 0
    wide_extra = extra.shape[1] if extra is not None else 0

    def kernel(base_ref, weight_ref, *refs):
        refs, out = list(refs[:-1]), refs[-1]
        for part in range(3):
            start = pl.multiple_of(part * (triple // 3) + base_ref[0] * columns, columns)
            out[:rows, part * columns : (part + 1) * columns] = weight_ref[:, pl.ds(start, columns)]
        if extra is not None:
            out[:rows, 3 * columns :] = refs.pop(0)[...]
        if below is not None:
            out[rows:, :] = jnp.zeros((below_rows, 3 * columns + wide_extra), LOW)
            out[rows:, : below.shape[1]] = refs.pop(0)[...]

    arrays = [attention_in] + [a for a in (extra, below) if a is not None]
    outs = [shape((rows + below_rows, 3 * columns + wide_extra), LOW)]
    return call(kernel, outs, [base], arrays)[0]


def join_slab(found, rows, parts, at_wide, below=0):
    across, beside = found
    pieces = [p for pair in zip(across, beside) for p in pair]
    count = len(pieces)

    def kernel(base_ref, *refs):
        for k in range(count):
            start = pl.multiple_of((base_ref[0] ^ k) * rows, rows)
            at = 0
            for i, columns in enumerate(parts):
                refs[count + i][pl.ds(start, rows), :] = refs[k][:rows, at : at + columns]
                at += columns
            if below:
                start = pl.multiple_of((base_ref[0] ^ k) * below, below)
                refs[-1][pl.ds(start, below), :] = refs[k][rows:, :rows]

    outs = [shape((count * rows, columns), LOW) for columns in parts]
    if below:
        outs.append(shape((count * below, rows), LOW))
    return call(kernel, outs, [at_wide], pieces)


def spread_columns(pieces, base):
    count, (rows, triple) = len(pieces), pieces[0].shape
    columns = triple // 3

    def kernel(base_ref, *refs):
        for k in range(count):
            for part in range(3):
                start = part * count * columns + (base_ref[0] ^ k) * columns
                refs[count][:, pl.ds(pl.multiple_of(start, columns), columns)] = refs[k][
                    :, part * columns : (part + 1) * columns
                ].astype(F32)

    return call(kernel, [shape((rows, count * triple), F32)], [base], pieces)[0]


def reorder(whole, slots, at_wide, outward):
    count = whole.shape[0] // slots
    order = list(range(0, count, 2)) + list(range(1, count, 2))

    def kernel(base_ref, whole_ref, out_ref):
        for i, k in enumerate(order):
            start = pl.multiple_of((base_ref[0] ^ k) * slots, slots)
            if outward:
                out_ref[pl.ds(start, slots), :] = whole_ref[i * slots : (i + 1) * slots, :]
            else:
                out_ref[i * slots : (i + 1) * slots, :] = whole_ref[pl.ds(start, slots), :]

    return call(kernel, [shape(whole.shape, whole.dtype)], [at_wide], [whole])[0]


def outer_pair(pieces, grad_packed, context, grad_attended):
    count, (slots, features) = len(pieces), pieces[0].shape
    columns = grad_packed.shape[1]

    def kernel(*refs):
        left = jnp.concatenate([r[...] for r in refs[:count]], axis=0)
        packed_ref, context_ref, attended_ref, out = refs[count:]
        out[:, :columns] = low(product(left, packed_ref[...], 0, 0))
        out[:, columns:] = low(product(context_ref[...], attended_ref[...], 0, 0))

    outs = [shape((features, columns + context.shape[1]), LOW)]
    flops = 2 * slots * features * (count * columns + context.shape[1])
    arrays = list(pieces) + [grad_packed, context, grad_attended]
    return call(kernel, outs, [], arrays, flops=flops)[0]


def stack_own(dense, pair, columns):
    units, features = dense.shape
    rows = pair.shape[0]

    def kernel(dense_ref, pair_ref, out_ref):
        out_ref[:units, :] = dense_ref[...]
        out_ref[units : units + rows, :] = pair_ref[:, columns:]
        out_ref[units + rows :, columns:] = jnp.zeros((rows, features - columns), LOW)
        out_ref[units + rows :, :columns] = pair_ref[:, :columns]

    return call(kernel, [shape((units + 2 * rows, features), LOW)], [], [dense, pair])[0]


def split_gathered(gathered, rows, columns):
    narrow = lax.axis_size("narrow")
    features = gathered.shape[1]
    block = gathered.shape[0] // narrow
    units = block - 2 * rows
    half = units * narrow // 2
    fold = features // half
    third = columns // 3

    def kernel(whole_ref, up_ref, down_ref, in_ref, out_ref):
        total = None
        for j in range(narrow):
            own = whole_ref[j * block : j * block + units, :].astype(F32)
            if j < narrow // 2:
                for i in range(fold):
                    at = i * half + j * units
                    up_ref[at : at + units, :] = own[:, i * half : (i + 1) * half]
            else:
                at = (j - narrow // 2) * units
                down_ref[at : at + units, :] = own
            at = j * block + units
            found = whole_ref[at : at + rows, :].astype(F32)
            total = found if total is None else total + found
            at += rows
            for part in range(3):
                start = part * narrow * third + j * third
                in_ref[:, start : start + third] = whole_ref[
                    at : at + rows, part * third : (part + 1) * third
                ].astype(F32)
        out_ref[...] = total

    outs = [
        shape((features, half), F32), shape((half, features), F32),
        shape((rows, narrow * columns), F32), shape((rows, features), F32),
    ]
    return call(kernel, outs, [], [gathered])


def dense_products(parts):
    return low(up_product(parts)), low(down_product(parts))


def dense_join(parts):
    up, down = parts
    features, units = up.shape
    fold = features // units

    def kernel(up_ref, down_ref, out_ref):
        for i in range(fold):
            out_ref[:units, i * units : (i + 1) * units] = up_ref[i * units : (i + 1) * units, :]
        out_ref[units:, :] = down_ref[...]

    return call(kernel, [shape((2 * units, features), LOW)], [], [up, down])[0]


def narrow_scatter(whole):
    return lax.psum_scatter(whole, "narrow", scatter_dimension=0, tiled=True)


def narrow_gather(own):
    return lax.all_gather(own, "narrow", axis=0, tiled=True)


def dense_outputs(gathered):
    units, features = gathered.shape[0] // 2, gathered.shape[1]
    fold = features // units

    def kernel(whole_ref, up_ref, down_ref):
        for i in range(fold):
            up_ref[i * units : (i + 1) * units, :] = whole_ref[
                :units, i * units : (i + 1) * units
            ].astype(F32)
        down_ref[...] = whole_ref[units:, :].astype(F32)

    return call(kernel, [shape((features, units), F32), shape((units, features), F32)], [], [gathered])


def gather_wide(own):
    return lax.all_gather(own, "wide", axis=0, tiled=True)


def after(value, *others):
    return lax.optimization_barrier((value,) + others)[0]


def reversed_order(count):
    bits = count.bit_length() - 1
    return [sum((i >> b & 1) << (bits - 1 - b) for b in range(bits)) for i in range(count)]


def outer_halves(lefts, right, base):
    count = len(lefts)
    wide = lax.axis_size("wide")
    slots, features = lefts[0].shape
    columns = right.shape[1]
    rows = features // wide
    order = reversed_order(wide)

    def kernel(base_ref, *refs):
        right_ref, keep_ref, send_ref, total_ref = refs[count:]
        left = refs[0][...] if count == 1 else jnp.concatenate([r[...] for r in refs[:count]], axis=0)
        total_ref[...] = product(left, right_ref[...], 0, 0)
        for i, k in enumerate(order):
            start = pl.multiple_of((base_ref[0] ^ k) * rows, rows)
            out, at = (keep_ref, i) if i < wide // 2 else (send_ref, i - wide // 2)
            out[at * rows : (at + 1) * rows, :] = low(total_ref[pl.ds(start, rows), :])

    outs = [shape((features // 2, columns), LOW)] * 2
    scratch = [pltpu.VMEM((features, columns), F32)]
    flops = 2 * count * slots * features * columns
    return call(kernel, outs, [base], list(lefts) + [right], scratch, flops)


def pair_sum(own, received, slots):
    count = own.shape[0] // slots
    features = own.shape[1]

    def kernel(own_ref, received_ref, *outs):
        for k in range(count):
            at = slice(k * slots, (k + 1) * slots)
            total = own_ref[at, :] + received_ref[at, :].astype(F32)
            outs[k][...] = total if k == 0 else low(total)

    outs = [shape((slots, features), F32)] + [shape((slots, features), LOW)] * (count - 1)
    return call(kernel, outs, [], [own, received])


def halving_step(halves, distance):
    keep, send = halves
    total = keep.astype(F32) + swap(send, "wide", distance).astype(F32)
    if 2 * distance == lax.axis_size("wide"):
        return total
    half = total.shape[0] // 2
    return total[:half], low(total[half:])


def halving_rest(halves, distance):
    while distance < lax.axis_size("wide"):
        halves = halving_step(halves, distance)
        distance *= 2
    return halves


def together(value, other):
    return lax.optimization_barrier((value, other))


def narrow_sum(value, first):
    narrow = lax.axis_size("narrow")
    bits = narrow.bit_length() - 1
    for b in range(bits):
        value = value + swap(low(value), "narrow", 1 << (b + first) % bits).astype(F32)
    return value


def axis_sum(value, axis, distance=1):
    while distance < lax.axis_size(axis):
        value = value + swap(value, axis, distance)
        distance *= 2
    return value


def layer_norm(source, gain):
    centre = source - jnp.mean(source, axis=-1, keepdims=True)
    inverse = lax.rsqrt(jnp.mean(centre * centre, axis=-1, keepdims=True) + 1e-05)
    scaled = centre * inverse
    return scaled * gain, scaled, inverse


def norm_back(upstream, scaled, inverse, gain):
    grad_scaled = upstream * gain
    mean_first = jnp.mean(grad_scaled, axis=-1, keepdims=True)
    mean_second = jnp.mean(grad_scaled * scaled, axis=-1, keepdims=True)
    return (
        inverse * (grad_scaled - mean_first - scaled * mean_second),
        jnp.sum(upstream * scaled, axis=0),
    )


def activate(source):
    return jax.nn.gelu(source)


def activation_back(source, upstream):
    return jax.vjp(activate, source)[1](upstream)[0]


def masked_scores(queries, keys, allowed):
    scores = product(queries, keys, 1, 1) * HEAD_DIM ** (-0.5)
    return jnp.where(allowed, scores, -1e30)


def allowed_of(length, slots):
    rows_at = lax.broadcasted_iota(jnp.int32, (slots, slots), 0)
    cols_at = lax.broadcasted_iota(jnp.int32, (slots, slots), 1)
    return (cols_at <= rows_at) & (cols_at < length)


def head_parts(packed, head, columns):
    return [
        packed[:, part * columns + head * HEAD_DIM : part * columns + (head + 1) * HEAD_DIM]
        for part in range(3)
    ]


def attention(pieces, gain, weight, lengths):
    count, (slots, features) = len(pieces), pieces[0].shape
    columns = weight.shape[1] // 3
    raw = gain is not None

    def kernel(lengths_ref, *refs):
        ins, weight_ref, refs = refs[:count], refs[count], refs[count + 1 :]
        if raw:
            gain_ref, refs = refs[0], refs[1:]
        packed_ref, level_ref, outs = refs[0], refs[1], refs[2 : count + 2]
        levels = []
        for j in range(count):
            if raw:
                rows = low(layer_norm(ins[j][...].astype(F32), gain_ref[...])[0])
                refs[count + 2 + j][...] = rows
            else:
                rows = ins[j][...]
            packed = low(product(rows, weight_ref[...], 1, 0))
            packed_ref[j] = packed
            allowed = allowed_of(lengths_ref[j], slots)
            found = []
            for head in range(columns // HEAD_DIM):
                queries, keys, values = head_parts(packed, head, columns)
                scores = masked_scores(queries, keys, allowed)
                top = jnp.max(scores, axis=-1, keepdims=True)
                raised = jnp.exp(scores - top)
                weight_sum = jnp.sum(raised, axis=-1, keepdims=True)
                levels.append(top + jnp.log(weight_sum))
                found.append(product(low(raised / weight_sum), values, 1, 0))
            outs[j][...] = low(jnp.concatenate(found, axis=1))
        level_ref[...] = jnp.concatenate(levels, axis=1)

    outs = [shape((count, slots, 3 * columns), LOW)]
    outs += [shape((slots, count * columns // HEAD_DIM), F32)]
    outs += [shape((slots, columns), LOW)] * count
    arrays = list(pieces) + [weight]
    if raw:
        outs += [shape((slots, features), LOW)] * count
        arrays.append(gain[None])
    flops = 2 * count * slots * features * 3 * columns
    packed, levels, *found = call(kernel, outs, [lengths], arrays, flops=flops)
    return (packed, levels), found[:count], found[count:] if raw else pieces


def attention_back(packed, grads, lengths):
    packed, levels = packed
    count, (slots, columns) = len(grads), grads[0].shape
    scaling = HEAD_DIM ** (-0.5)

    def kernel(lengths_ref, packed_ref, level_ref, *refs):
        out = refs[count]
        for j in range(count):
            allowed = allowed_of(lengths_ref[j], slots)
            whole = packed_ref[j]
            grad_whole = refs[j][...]
            found = [[], [], []]
            for head in range(columns // HEAD_DIM):
                queries, keys, values = head_parts(whole, head, columns)
                grad_head = grad_whole[:, head * HEAD_DIM : (head + 1) * HEAD_DIM]
                at = j * (columns // HEAD_DIM) + head
                scores = masked_scores(queries, keys, allowed)
                softened = jnp.exp(scores - level_ref[:, at : at + 1])
                grad_soft = product(grad_head, values, 1, 1)
                inner = jnp.sum(softened * grad_soft, axis=-1, keepdims=True)
                grad_scores = low(softened * (grad_soft - inner))
                found[0].append(scaling * product(grad_scores, keys, 1, 0))
                found[1].append(scaling * product(grad_scores, queries, 0, 0))
                found[2].append(product(low(softened), grad_head, 0, 0))
            out[j * slots : (j + 1) * slots, :] = low(
                jnp.concatenate(found[0] + found[1] + found[2], axis=1)
            )

    outs = [shape((count * slots, 3 * columns), LOW)]
    return call(kernel, outs, [lengths], [packed, levels] + list(grads))[0]


def normed_back(grad_packed, weight, count):
    slots, features = grad_packed.shape[0] // count, weight.shape[0]

    def kernel(grad_ref, weight_ref, *outs):
        whole = low(product(grad_ref[...], weight_ref[...], 1, 1))
        for j in range(count):
            outs[j][...] = whole[j * slots : (j + 1) * slots]

    outs = [shape((slots, features), LOW)] * count
    flops = 2 * count * slots * features * weight.shape[1]
    return call(kernel, outs, [], [grad_packed, weight], flops=flops)


def wide_across(own):
    return [own] + [swap(own, "wide", apart) for apart in range(2, lax.axis_size("wide"), 2)]


def wide_pieces(own):
    across = wide_across(own)
    return across, [swap(piece, "wide", 1) for piece in across]


def wide_join(pieces):
    across, beside = pieces
    return join_rows(list(across) + list(beside))


def wide_sends(own, received, slots):
    parts = pair_sum(own, received, slots)
    return [parts[0]] + [swap(p, "wide", 2 * (i + 1)) for i, p in enumerate(parts[1:])]


def wide_total(parts):
    total = parts[0]
    for part in parts[1:]:
        total = total + part.astype(F32)
    return total


def wide_sums(halves, slots):
    own, other = halves
    return wide_total(wide_sends(own, swap(other, "wide", 1), slots))


def place(labels, experts, capacity):
    blocks, slots = labels.shape
    first = jnp.arange(blocks, dtype=jnp.int32)[:, None] * capacity - 1
    places = jnp.arange(blocks * capacity, dtype=jnp.int32)
    selects = []
    for expert in experts:
        chosen = labels == expert
        at = jnp.where(chosen, first + jnp.cumsum(chosen.astype(jnp.int32), axis=1), -1)
        selects.append(low(places[:, None] == at.reshape(-1)[None, :]))
    return selects


def picked(selects, rows):
    return [low(product(select, rows, 1, 0)) for select in selects]


def exchanged(sent, slices):
    narrow = lax.axis_size("narrow")
    return join_rows(
        [sent[j // slices] if j == 0 else swap(sent[j // slices], "narrow", j) for j in range(narrow)]
    )


def to_experts(selects, rows, slices):
    return exchanged(picked(selects, rows), slices)


def from_experts(selects, outcome, slices):
    narrow = lax.axis_size("narrow")
    parts = outcome.reshape(narrow, -1, outcome.shape[-1])
    found = []
    for r in range(len(selects)):
        total = None
        for j in range(r * slices, (r + 1) * slices):
            part = parts[j] if j == 0 else swap(low(parts[j]), "narrow", j).astype(F32)
            total = part if total is None else total + part
        found.append(low(total))
    return found


def spread_of(selects, found, at):
    total = None
    for select, rows in zip(selects, found):
        part = product(select[:, at], rows, 0, 0)
        total = part if total is None else total + part
    return total


def layer_forward(source, raw, weights, selects, lengths, at_narrow, slices, second_work=None, third_work=None):
    norm_first, attention_in, attention_out, norm_second, mixer, up, down, expert_up, expert_down = weights
    slots, features = source.shape
    wide, narrow = lax.axis_size("wide"), lax.axis_size("narrow")
    normed, scaled_one, inverse_one = layer_norm(source, norm_first)
    own = low(normed)
    pieces = raw
    if raw is None:
        pieces = [own] + [swap(own, "narrow", j) for j in range(1, narrow)]
    packed, contexts, pieces = attention(
        pieces, None if raw is None else norm_first, attention_in, lengths
    )
    context, middle, second, scaled_two, inverse_two = attended(
        [contexts[0]] + [swap(contexts[j], "narrow", j) for j in range(1, narrow)],
        attention_out, source, norm_second, at_narrow,
    )
    across, beside = wide_pieces(second)
    if second_work is not None:
        across, second_found = together(across, second_work(second))
    rows = wide_join((across, beside))
    mixing = jax.nn.softmax(jnp.dot(rows, mixer, preferred_element_type=F32), axis=-1)
    pre = jnp.dot(rows, up, preferred_element_type=F32)
    act = low(activate(pre))
    third_found = None if third_work is None else third_work(rows, second_found)
    expert_rows, (mixing, pre, act, third_found) = together(
        to_experts(selects, rows, slices), (mixing, pre, act, third_found)
    )
    expert_pre = jnp.dot(expert_rows, expert_up, preferred_element_type=F32)
    expert_act = low(activate(expert_pre))
    kept = (
        scaled_one, inverse_one, pieces, packed, context, scaled_two, inverse_two,
        (rows, mixing, expert_rows, expert_pre, expert_act, pre, act),
    )
    return (middle, kept) if second_work is None else (middle, kept, third_found)


def experts_found(kept, weights, selects, slices, gate=None):
    act = kept[7][4] if gate is None else after(kept[7][4], gate)
    outcome = jnp.dot(act, weights[8], preferred_element_type=F32)
    return from_experts(selects, outcome, slices)


def merged_halves(kept, weights, selects, found, slots):
    mixing, act = kept[7][1], kept[7][6]

    def merged(at):
        dense = jnp.dot(act[at], weights[6], preferred_element_type=F32)
        return mixing[at, :1] * dense + mixing[at, 1:] * spread_of(selects, found, at)

    half = act.shape[0] // 2
    return merged(slice(0, half)), low(merged(slice(half, 2 * half)))


def dense_back_of(through, kept, weights):
    rows, mixing, _, _, _, pre, act = kept[7]
    dense_dot = jnp.sum(act.astype(F32) * through, axis=1, keepdims=True)
    dense_logit = mixing[:, :1] * mixing[:, 1:] * dense_dot
    grad_pre = low(activation_back(pre, mixing[:, :1] * through))
    return grad_pre, dense_logit


def experts_back(upstream, gathered, kept, weights, selects, slices, beneath, alongside):
    norm_second, mixer, up, down, expert_up, expert_down = weights[3:]
    scaled_two, inverse_two = kept[5:7]
    rows, mixing, expert_rows, expert_pre, expert_act, pre, act = kept[7]
    slots = upstream.shape[0]
    wide = lax.axis_size("wide")
    mixer_gap = (mixer[:, 0].astype(F32) - mixer[:, 1].astype(F32))[None]
    grads, expert_grads, through, dense_back = gathered
    expert_mixing = jax.nn.softmax(
        jnp.dot(expert_rows, mixer, preferred_element_type=F32), axis=-1
    )
    expert_dot = jnp.sum(expert_act.astype(F32) * through, axis=1, keepdims=True)
    expert_logit = -expert_mixing[:, :1] * expert_mixing[:, 1:] * expert_dot
    expert_grad_pre = low(activation_back(expert_pre, expert_mixing[:, 1:] * through))
    expert_back = product(expert_grad_pre, expert_up, 1, 1) + expert_logit * mixer_gap
    if callable(dense_back):
        dense_back = dense_back(expert_back)
    grad_pre, dense_logit = dense_back
    dense = (rows, grad_pre, act, mixing[:, :1], grads)
    found = from_experts(selects, expert_back, slices)
    experts = (
        expert_rows, expert_grad_pre,
        expert_act, expert_mixing[:, 1:], expert_grads,
    )
    found, beneath_found = together(found, beneath(expert_back, experts, dense))

    def merged(at):
        dense_back = product(grad_pre[at], up, 1, 1) + dense_logit[at] * mixer_gap
        return dense_back + spread_of(selects, found, at)

    half = grad_pre.shape[0] // 2
    halves = merged(slice(0, half)), low(merged(slice(half, 2 * half)))
    parts = wide_sends(halves[0], swap(halves[1], "wide", 1), slots)
    rows, dense_logit, expert_rows, expert_logit = after(
        (rows, dense_logit, expert_rows, expert_logit), parts[0]
    )
    grad_gap = jnp.sum(rows.astype(F32) * dense_logit, axis=0) + jnp.sum(
        expert_rows.astype(F32) * expert_logit, axis=0
    )
    grad_second, (grad_gap, alongside_found) = together(
        wide_total(parts), (grad_gap, alongside(parts[0], halves[1], beneath_found, experts, dense))
    )
    grad_norm_part, grad_norm_second = norm_back(grad_second, scaled_two, inverse_two, norm_second)
    return (
        upstream + grad_norm_part, dense, experts, (grad_norm_second, grad_gap),
        beneath_found, alongside_found,
    )


def up_product(parts):
    return product(parts[0], parts[1], 0, 0)


def down_product(parts):
    act, mix, grads = parts[2:]
    return product(act, low(mix * grads.astype(F32)), 0, 0)


def attention_grads(grad_middle, kept, weights, lengths, at_narrow, hold, filler):
    norm_first, attention_in, attention_out = weights[:3]
    scaled_one, inverse_one, pieces, packed, context = kept[:5]
    narrow = lax.axis_size("narrow")
    grad_attended = low(grad_middle)
    grad_contexts = context_back(grad_attended, attention_out, narrow, at_narrow)
    grad_contexts = [grad_contexts[0]] + [
        swap(grad_contexts[j], "narrow", j) for j in range(1, narrow)
    ]
    grad_packed = attention_back(packed, grad_contexts, lengths)
    grad_packed, hold = together(grad_packed, hold)
    parts = normed_back(grad_packed, attention_in, narrow)
    weight_grads = (pieces, after(grad_packed, parts), context, grad_attended)
    filled = filler(parts[0])
    parts = [parts[0]] + [swap(parts[j], "narrow", j) for j in range(1, narrow)]
    parts, filled = together(parts, filled)
    grad_normed = sum(part.astype(F32) for part in parts)
    grad_norm_part, grad_norm_first = norm_back(grad_normed, scaled_one, inverse_one, norm_first)
    return grad_middle + grad_norm_part, grad_norm_first, weight_grads, hold, filled


def last_grads(
    grad_middle, kept, weights, lengths, at_narrow, at_wide, dense, pair, narrow_columns, early
):
    norm_first, attention_in, attention_out = weights[:3]
    scaled_one, inverse_one, pieces, packed, context = kept[:5]
    narrow = lax.axis_size("narrow")
    grad_attended = low(grad_middle)
    grad_contexts = context_back(grad_attended, attention_out, narrow, at_narrow)
    grad_contexts = [grad_contexts[0]] + [
        swap(grad_contexts[j], "narrow", j) for j in range(1, narrow)
    ]
    out_halves = outer_halves([context], after(grad_attended, grad_contexts[-1]), at_wide)
    grad_contexts, out_halves = together(grad_contexts, halving_step(out_halves, 1))
    rows = pair.shape[0]
    gathered = narrow_gather(stack_own(dense, after(pair, grad_contexts), narrow_columns))
    out_halves = halving_step(out_halves, 2)
    early = after(early, grad_contexts)
    early = early + swap(early, "narrow", 1)
    grad_packed = attention_back(packed, grad_contexts, lengths)
    grad_packed, (out_halves, early) = together(grad_packed, (out_halves, early))
    in_halves = outer_halves(pieces, grad_packed, at_wide)
    in_halves, early = together(in_halves, axis_sum(early, "narrow", 2))
    parts = normed_back(after(grad_packed, in_halves), attention_in, narrow)
    in_halves = halving_step(halving_step(in_halves, 1), 2)
    parts = [parts[0]] + [swap(parts[j], "narrow", j) for j in range(1, narrow)]
    parts = after(parts, in_halves)
    grad_normed = sum(part.astype(F32) for part in parts)
    grad_norm_part, grad_norm_first = norm_back(grad_normed, scaled_one, inverse_one, norm_first)
    grad_inputs = grad_middle + grad_norm_part
    out_sum = halving_rest(out_halves, 4)
    in_sum, (first, grad_inputs) = together(
        low(halving_rest(in_halves, 4)), (grad_norm_first[None], grad_inputs)
    )
    out_sum = after(out_sum, in_halves)
    out_sum = out_sum + swap(low(out_sum), "narrow", 1).astype(F32)
    in_pieces = [in_sum] + [swap(in_sum, "narrow", j) for j in range(1, narrow)]
    in_pieces, gathered = together(
        in_pieces, split_gathered(after(gathered, in_sum), rows, narrow_columns)
    )
    vectors = axis_sum(jnp.concatenate([axis_sum(first, "narrow"), early], axis=0), "wide")
    spread = spread_columns(in_pieces, at_narrow)
    out_sum = after(out_sum, in_sum)
    distance = 2
    while distance < narrow:
        received = swap(low(out_sum), "narrow", distance)
        distance *= 2
        if distance >= narrow:
            received = after(received, spread)
        out_sum = out_sum + received.astype(F32)
    return grad_inputs, (spread, out_sum), vectors, gathered


def body(
    inputs, cotangent, seq_len, shallow_routes, deep_routes,
    shallow_norm_first, shallow_attention_in, shallow_attention_out, shallow_norm_second,
    shallow_dense_up, shallow_dense_down, shallow_mixer, shallow_expert_up, shallow_expert_down,
    deep_norm_first, deep_attention_in, deep_attention_out, deep_norm_second,
    deep_dense_up, deep_dense_down, deep_mixer, deep_expert_up, deep_expert_down,
):
    wide, narrow = lax.axis_size("wide"), lax.axis_size("narrow")
    wide_at, narrow_at = lax.axis_index("wide"), lax.axis_index("narrow")
    at_wide, at_narrow = wide_at.reshape(1), narrow_at.reshape(1)
    slots, features = inputs.shape
    small = jnp.stack(
        [
            shallow_norm_first, shallow_norm_second, deep_norm_first, deep_norm_second,
            shallow_mixer[:, 0], shallow_mixer[:, 1], deep_mixer[:, 0], deep_mixer[:, 1],
        ]
    )
    narrow_columns = 3 * features // narrow
    rows_own = shallow_attention_in.shape[0]
    input_pieces = [inputs] + [swap(inputs, "narrow", j) for j in range(1, narrow)]
    across = wide_across(own_slab(shallow_attention_in, None, at_narrow, small))
    lengths = seq_len[wide_at * narrow + (narrow_at ^ jnp.arange(narrow))]
    deep_slab = own_slab(deep_attention_in, None, at_narrow, None)
    across, (input_pieces, lengths, deep_slab) = together(
        across, (input_pieces, lengths, deep_slab)
    )
    in_pieces = across, [swap(piece, "wide", 1) for piece in across]
    shallow_in, small = join_slab(
        in_pieces, rows_own, [narrow_columns], at_wide, small.shape[0]
    )
    shallow_out = gather_wide(after(shallow_attention_out, in_pieces[0][-1]))
    small = jnp.transpose(small.reshape(wide, 8, -1), (1, 0, 2)).reshape(8, features)
    gains = small[:4].astype(F32)
    def selects_of(routes, slices):
        table = routes.reshape(wide, narrow, slots)
        own = lax.dynamic_index_in_dim(table, narrow_at, axis=1, keepdims=False)
        capacity = slices * max(1, 3 * slots // (2 * wide * narrow))
        groups = narrow // slices
        experts = [wide_at * groups + ((narrow_at // slices) ^ r) for r in range(groups)]
        order = jnp.array(list(range(0, wide, 2)) + list(range(1, wide, 2)))
        return place(own[wide_at ^ order], experts, capacity)

    shallow_selects = selects_of(shallow_routes, SLICES_SHALLOW)
    deep_selects = selects_of(deep_routes, SLICES_DEEP)
    shallow = (
        gains[0], shallow_in, shallow_out, gains[1], small[4:6].T,
        shallow_dense_up, shallow_dense_down, shallow_expert_up[0], shallow_expert_down[0],
    )
    middle, kept_shallow = layer_forward(
        inputs.astype(F32), input_pieces, shallow, shallow_selects, lengths, at_narrow, SLICES_SHALLOW
    )
    deep_in = gather_wide(after(deep_slab, kept_shallow[7][0]))
    deep_out = gather_wide(after(deep_attention_out, kept_shallow[7][2]))
    found = experts_found(kept_shallow, shallow, shallow_selects, SLICES_SHALLOW)
    halves = merged_halves(kept_shallow, shallow, shallow_selects, found, slots)
    total = wide_sums(halves, slots)
    passed = middle + total
    all_grads = gather_wide(after(cotangent, total))
    deep = (
        gains[2], deep_in, deep_out, gains[3], small[6:8].T,
        deep_dense_up, deep_dense_down, deep_expert_up[0], deep_expert_down[0],
    )
    def second_work(second):
        grads = reorder(after(all_grads, second), slots, at_wide, False)
        expert_grads = to_experts(deep_selects, grads, SLICES_DEEP)
        return grads, expert_grads, product(grads, deep_dense_down, 1, 1)

    def third_work(rows, found):
        grads, expert_grads, through = found
        return grads, expert_grads, through, product(after(expert_grads, rows), deep_expert_down[0], 1, 1)

    middle, kept_deep, gathered = layer_forward(
        passed, None, deep, deep_selects, lengths, at_narrow, SLICES_DEEP, second_work, third_work
    )
    def deep_result(found):
        halves = merged_halves(kept_deep, deep, deep_selects, found, slots)
        return reorder(
            jnp.concatenate([low(halves[0]), halves[1]], axis=0), slots, at_wide, True
        )

    grad_middle, _, deep_experts, deep_rows, (whole, found), result = experts_back(
        cotangent.astype(F32),
        gathered[:2] + (
            gathered[3],
            lambda token: dense_back_of(after(gathered[2], token), kept_deep, deep),
        ), kept_deep,
        deep, deep_selects, SLICES_DEEP,
        lambda token, experts, dense: (
            dense_join(dense_products(after(dense, token))),
            experts_found(kept_deep, deep, deep_selects, SLICES_DEEP, token),
        ),
        lambda token, other, found, experts, dense: deep_result(after(found[1], token)),
    )
    total = lax.psum_scatter(result, "wide", scatter_dimension=0, tiled=True)
    grad_passed, deep_first, outer_parts, whole, deep_down = attention_grads(
        grad_middle, kept_deep, deep, lengths, at_narrow, narrow_scatter(whole),
        lambda token: down_product(after(deep_experts, token)),
    )
    passed_low = low(grad_passed)
    across, beside = wide_pieces(passed_low)
    across, total = together(across, total)
    grads = wide_join((across, beside))
    pair = outer_pair(*after(outer_parts, grads))
    expert_grads, (pair, dense_back) = together(
        to_experts(shallow_selects, grads, SLICES_SHALLOW),
        (
            pair,
            dense_back_of(product(grads, shallow_dense_down, 1, 1), kept_shallow, shallow),
        ),
    )
    pair = lax.psum_scatter(pair, "wide", scatter_dimension=0, tiled=True)
    whole = narrow_gather(after(whole, passed_low))
    grad_middle, _, _, shallow_rows, (joined, deep_up), (shallow_experts, pair, deep_dense) = experts_back(
        grad_passed,
        (grads, expert_grads, product(expert_grads, shallow_expert_down[0], 1, 1), dense_back),
        kept_shallow, shallow, shallow_selects, SLICES_SHALLOW,
        lambda token, experts, dense: (
            dense_join(dense_products(after(dense, token))),
            up_product(after(deep_experts, token)),
        ),
        lambda token, other, found, experts, dense: (
            [f(after(experts, token)) for f in (up_product, down_product)], pair,
            dense_outputs(after(whole, token)),
        ),
    )
    shallow_up, shallow_down = shallow_experts
    early = jnp.stack(list(shallow_rows) + [deep_first] + list(deep_rows))
    grad_inputs, (grad_shallow_in, grad_shallow_out), vectors, gathered = last_grads(
        grad_middle, kept_shallow, shallow, lengths, at_narrow, at_wide,
        narrow_scatter(joined), pair, narrow_columns, early,
    )
    *shallow_dense, grad_deep_in, grad_deep_out = gathered
    output = middle + total.astype(F32)
    deep_up, deep_down = deep_up[None], deep_down[None]
    shallow_up, shallow_down = shallow_up[None], shallow_down[None]
    grads_shallow = (
        grad_shallow_in, grad_shallow_out, *shallow_dense, shallow_up, shallow_down,
    )
    grads_deep = (
        grad_deep_in, grad_deep_out, *deep_dense, deep_up, deep_down,
    )
    vectors = lax.dynamic_slice_in_dim(vectors, wide_at * (features // wide), features // wide, axis=1)

    def outputs_of(grads, rows):
        grad_mixer = jnp.stack([rows[2], -rows[2]], axis=1)
        return (
            rows[0], grads[0], grads[1], rows[1], grads[2], grads[3], grad_mixer, grads[4], grads[5],
        )

    return (
        (low(output), grad_inputs)
        + outputs_of(grads_shallow, vectors[:3])
        + outputs_of(grads_deep, vectors[3:])
    )


def solution(mesh):
    both = ("wide", "narrow")
    parameters = (
        P("wide"), P("wide", None), P("wide", None), P("wide"), P(None, "wide"),
        P("wide", None), P("wide", None), P(both, None, None), P(both, None, None),
    )
    return jax.shard_map(
        body,
        mesh=mesh,
        in_specs=(P(both, None), P(both, None), P(), P(), P()) + parameters + parameters,
        out_specs=(P(both, None), P(both, None)) + parameters + parameters,
        check_vma=False,
    )
```

```python
import jax
import jax.numpy as jnp
from jax import lax
from jax.experimental import pallas as pl
from jax.experimental.pallas import tpu as pltpu
from jax.sharding import PartitionSpec as P

HEAD_DIM = 64
SLICES_SHALLOW = 4
SLICES_DEEP = 2
F32 = jnp.float32
LOW = jnp.bfloat16
VMEM_LIMIT = 60 * 1024 * 1024


def low(value):
    return value.astype(LOW)


def swap(array, axis, distance):
    return lax.ppermute(array, axis, [(i, i ^ distance) for i in range(lax.axis_size(axis))])


def product(left, right, left_dim, right_dim):
    return lax.dot_general(
        left, right, (((left_dim,), (right_dim,)), ((), ())), preferred_element_type=F32
    )


def vmem():
    return pl.BlockSpec(memory_space=pltpu.VMEM)


def smem():
    return pl.BlockSpec(memory_space=pltpu.SMEM)


def call(kernel, outs, scalars, arrays, scratch=(), flops=0):
    moved = sum(a.size * a.dtype.itemsize for a in list(arrays) + list(outs))
    return pl.pallas_call(
        kernel,
        out_shape=tuple(outs),
        in_specs=[smem()] * len(scalars) + [vmem()] * len(arrays),
        out_specs=tuple(vmem() for _ in outs),
        scratch_shapes=list(scratch),
        compiler_params=pltpu.CompilerParams(vmem_limit_bytes=VMEM_LIMIT),
        cost_estimate=pl.CostEstimate(flops=flops, bytes_accessed=moved, transcendentals=0),
    )(*scalars, *arrays)


def shape(dims, kind):
    return jax.ShapeDtypeStruct(dims, kind)


def join_rows(pieces):
    if len(pieces) == 1:
        return pieces[0]
    count, (rows, columns) = len(pieces), pieces[0].shape

    def kernel(*refs):
        for k in range(count):
            refs[count][k * rows : (k + 1) * rows, :] = refs[k][...]

    return call(kernel, [shape((count * rows, columns), pieces[0].dtype)], [], pieces)[0]


def context_back(grads, weight, count, base):
    slots, features = grads.shape
    columns = features // count

    def kernel(base_ref, grads_ref, weight_ref, *outs):
        for k in range(count):
            start = pl.multiple_of((base_ref[0] ^ k) * columns, columns)
            outs[k][...] = low(product(grads_ref[...], weight_ref[pl.ds(start, columns), :], 1, 1))

    outs = [shape((slots, columns), LOW)] * count
    flops = 2 * slots * features * features
    return call(kernel, outs, [base], [grads, weight], flops=flops)


def attended(pieces, weight, source, gain, base):
    count, (slots, columns) = len(pieces), pieces[0].shape
    features = source.shape[1]

    def kernel(base_ref, weight_ref, source_ref, gain_ref, *refs):
        context_ref, middle_ref, second_ref, scaled_ref, inverse_ref = refs[count:]
        total = source_ref[...]
        for k in range(count):
            start = pl.multiple_of((base_ref[0] ^ k) * columns, columns)
            context_ref[:, pl.ds(start, columns)] = refs[k][...]
            total = total + product(refs[k][...], weight_ref[pl.ds(start, columns), :], 1, 0)
        middle_ref[...] = total
        second, scaled, inverse = layer_norm(total, gain_ref[...])
        second_ref[...] = low(second)
        scaled_ref[...] = scaled
        inverse_ref[...] = inverse

    outs = [
        shape((slots, features), LOW), shape((slots, features), F32), shape((slots, features), LOW),
        shape((slots, features), F32), shape((slots, 1), F32),
    ]
    flops = 2 * slots * features * features
    return call(kernel, outs, [base], [weight, source, gain[None]] + list(pieces), flops=flops)


def own_slab(attention_in, extra, base, below):
    rows, triple = attention_in.shape
    columns = triple // (3 * lax.axis_size("narrow"))
    below_rows = below.shape[0] if below is not None else 0
    wide_extra = extra.shape[1] if extra is not None else 0

    def kernel(base_ref, weight_ref, *refs):
        refs, out = list(refs[:-1]), refs[-1]
        for part in range(3):
            start = pl.multiple_of(part * (triple // 3) + base_ref[0] * columns, columns)
            out[:rows, part * columns : (part + 1) * columns] = weight_ref[:, pl.ds(start, columns)]
        if extra is not None:
            out[:rows, 3 * columns :] = refs.pop(0)[...]
        if below is not None:
            out[rows:, :] = jnp.zeros((below_rows, 3 * columns + wide_extra), LOW)
            out[rows:, : below.shape[1]] = refs.pop(0)[...]

    arrays = [attention_in] + [a for a in (extra, below) if a is not None]
    outs = [shape((rows + below_rows, 3 * columns + wide_extra), LOW)]
    return call(kernel, outs, [base], arrays)[0]


def join_slab(found, rows, parts, at_wide, below=0):
    across, beside = found
    pieces = [p for pair in zip(across, beside) for p in pair]
    count = len(pieces)

    def kernel(base_ref, *refs):
        for k in range(count):
            start = pl.multiple_of((base_ref[0] ^ k) * rows, rows)
            at = 0
            for i, columns in enumerate(parts):
                refs[count + i][pl.ds(start, rows), :] = refs[k][:rows, at : at + columns]
                at += columns
            if below:
                start = pl.multiple_of((base_ref[0] ^ k) * below, below)
                refs[-1][pl.ds(start, below), :] = refs[k][rows:, :rows]

    outs = [shape((count * rows, columns), LOW) for columns in parts]
    if below:
        outs.append(shape((count * below, rows), LOW))
    return call(kernel, outs, [at_wide], pieces)


def spread_columns(pieces, base):
    count, (rows, triple) = len(pieces), pieces[0].shape
    columns = triple // 3

    def kernel(base_ref, *refs):
        for k in range(count):
            for part in range(3):
                start = part * count * columns + (base_ref[0] ^ k) * columns
                refs[count][:, pl.ds(pl.multiple_of(start, columns), columns)] = refs[k][
                    :, part * columns : (part + 1) * columns
                ].astype(F32)

    return call(kernel, [shape((rows, count * triple), F32)], [base], pieces)[0]


def reorder(whole, slots, at_wide, outward):
    count = whole.shape[0] // slots
    order = list(range(0, count, 2)) + list(range(1, count, 2))

    def kernel(base_ref, whole_ref, out_ref):
        for i, k in enumerate(order):
            start = pl.multiple_of((base_ref[0] ^ k) * slots, slots)
            if outward:
                out_ref[pl.ds(start, slots), :] = whole_ref[i * slots : (i + 1) * slots, :]
            else:
                out_ref[i * slots : (i + 1) * slots, :] = whole_ref[pl.ds(start, slots), :]

    return call(kernel, [shape(whole.shape, whole.dtype)], [at_wide], [whole])[0]


def outer_pair(pieces, grad_packed, context, grad_attended):
    count, (slots, features) = len(pieces), pieces[0].shape
    columns = grad_packed.shape[1]

    def kernel(*refs):
        left = jnp.concatenate([r[...] for r in refs[:count]], axis=0)
        packed_ref, context_ref, attended_ref, out = refs[count:]
        out[:, :columns] = low(product(left, packed_ref[...], 0, 0))
        out[:, columns:] = low(product(context_ref[...], attended_ref[...], 0, 0))

    outs = [shape((features, columns + context.shape[1]), LOW)]
    flops = 2 * slots * features * (count * columns + context.shape[1])
    arrays = list(pieces) + [grad_packed, context, grad_attended]
    return call(kernel, outs, [], arrays, flops=flops)[0]


def stack_own(dense, pair, columns):
    units, features = dense.shape
    rows = pair.shape[0]

    def kernel(dense_ref, pair_ref, out_ref):
        out_ref[:units, :] = dense_ref[...]
        out_ref[units : units + rows, :] = pair_ref[:, columns:]
        out_ref[units + rows :, columns:] = jnp.zeros((rows, features - columns), LOW)
        out_ref[units + rows :, :columns] = pair_ref[:, :columns]

    return call(kernel, [shape((units + 2 * rows, features), LOW)], [], [dense, pair])[0]


def split_gathered(gathered, rows, columns):
    narrow = lax.axis_size("narrow")
    features = gathered.shape[1]
    block = gathered.shape[0] // narrow
    units = block - 2 * rows
    half = units * narrow // 2
    fold = features // half
    third = columns // 3

    def kernel(whole_ref, up_ref, down_ref, in_ref, out_ref):
        total = None
        for j in range(narrow):
            own = whole_ref[j * block : j * block + units, :].astype(F32)
            if j < narrow // 2:
                for i in range(fold):
                    at = i * half + j * units
                    up_ref[at : at + units, :] = own[:, i * half : (i + 1) * half]
            else:
                at = (j - narrow // 2) * units
                down_ref[at : at + units, :] = own
            at = j * block + units
            found = whole_ref[at : at + rows, :].astype(F32)
            total = found if total is None else total + found
            at += rows
            for part in range(3):
                start = part * narrow * third + j * third
                in_ref[:, start : start + third] = whole_ref[
                    at : at + rows, part * third : (part + 1) * third
                ].astype(F32)
        out_ref[...] = total

    outs = [
        shape((features, half), F32), shape((half, features), F32),
        shape((rows, narrow * columns), F32), shape((rows, features), F32),
    ]
    return call(kernel, outs, [], [gathered])


def dense_products(parts):
    return low(up_product(parts)), low(down_product(parts))


def dense_join(parts):
    up, down = parts
    features, units = up.shape
    fold = features // units

    def kernel(up_ref, down_ref, out_ref):
        for i in range(fold):
            out_ref[:units, i * units : (i + 1) * units] = up_ref[i * units : (i + 1) * units, :]
        out_ref[units:, :] = down_ref[...]

    return call(kernel, [shape((2 * units, features), LOW)], [], [up, down])[0]


def narrow_scatter(whole):
    return lax.psum_scatter(whole, "narrow", scatter_dimension=0, tiled=True)


def narrow_gather(own):
    return lax.all_gather(own, "narrow", axis=0, tiled=True)


def dense_outputs(gathered):
    units, features = gathered.shape[0] // 2, gathered.shape[1]
    fold = features // units

    def kernel(whole_ref, up_ref, down_ref):
        for i in range(fold):
            up_ref[i * units : (i + 1) * units, :] = whole_ref[
                :units, i * units : (i + 1) * units
            ].astype(F32)
        down_ref[...] = whole_ref[units:, :].astype(F32)

    return call(kernel, [shape((features, units), F32), shape((units, features), F32)], [], [gathered])


def gather_wide(own):
    return lax.all_gather(own, "wide", axis=0, tiled=True)


def after(value, *others):
    return lax.optimization_barrier((value,) + others)[0]


def reversed_order(count):
    bits = count.bit_length() - 1
    return [sum((i >> b & 1) << (bits - 1 - b) for b in range(bits)) for i in range(count)]


def outer_halves(lefts, right, base):
    count = len(lefts)
    wide = lax.axis_size("wide")
    slots, features = lefts[0].shape
    columns = right.shape[1]
    rows = features // wide
    order = reversed_order(wide)

    def kernel(base_ref, *refs):
        right_ref, keep_ref, send_ref, total_ref = refs[count:]
        left = refs[0][...] if count == 1 else jnp.concatenate([r[...] for r in refs[:count]], axis=0)
        total_ref[...] = product(left, right_ref[...], 0, 0)
        for i, k in enumerate(order):
            start = pl.multiple_of((base_ref[0] ^ k) * rows, rows)
            out, at = (keep_ref, i) if i < wide // 2 else (send_ref, i - wide // 2)
            out[at * rows : (at + 1) * rows, :] = low(total_ref[pl.ds(start, rows), :])

    outs = [shape((features // 2, columns), LOW)] * 2
    scratch = [pltpu.VMEM((features, columns), F32)]
    flops = 2 * count * slots * features * columns
    return call(kernel, outs, [base], list(lefts) + [right], scratch, flops)


def pair_sum(own, received, slots):
    count = own.shape[0] // slots
    features = own.shape[1]

    def kernel(own_ref, received_ref, *outs):
        for k in range(count):
            at = slice(k * slots, (k + 1) * slots)
            total = own_ref[at, :] + received_ref[at, :].astype(F32)
            outs[k][...] = total if k == 0 else low(total)

    outs = [shape((slots, features), F32)] + [shape((slots, features), LOW)] * (count - 1)
    return call(kernel, outs, [], [own, received])


def halving_step(halves, distance):
    keep, send = halves
    total = keep.astype(F32) + swap(send, "wide", distance).astype(F32)
    if 2 * distance == lax.axis_size("wide"):
        return total
    half = total.shape[0] // 2
    return total[:half], low(total[half:])


def halving_rest(halves, distance):
    while distance < lax.axis_size("wide"):
        halves = halving_step(halves, distance)
        distance *= 2
    return halves


def together(value, other):
    return lax.optimization_barrier((value, other))


def narrow_sum(value, first):
    narrow = lax.axis_size("narrow")
    bits = narrow.bit_length() - 1
    for b in range(bits):
        value = value + swap(low(value), "narrow", 1 << (b + first) % bits).astype(F32)
    return value


def axis_sum(value, axis, distance=1):
    while distance < lax.axis_size(axis):
        value = value + swap(value, axis, distance)
        distance *= 2
    return value


def layer_norm(source, gain):
    centre = source - jnp.mean(source, axis=-1, keepdims=True)
    inverse = lax.rsqrt(jnp.mean(centre * centre, axis=-1, keepdims=True) + 1e-05)
    scaled = centre * inverse
    return scaled * gain, scaled, inverse


def norm_back(upstream, scaled, inverse, gain):
    grad_scaled = upstream * gain
    mean_first = jnp.mean(grad_scaled, axis=-1, keepdims=True)
    mean_second = jnp.mean(grad_scaled * scaled, axis=-1, keepdims=True)
    return (
        inverse * (grad_scaled - mean_first - scaled * mean_second),
        jnp.sum(upstream * scaled, axis=0),
    )


def activate(source):
    return jax.nn.gelu(source)


def activation_back(source, upstream):
    return jax.vjp(activate, source)[1](upstream)[0]


def masked_scores(queries, keys, allowed):
    scores = product(queries, keys, 1, 1) * HEAD_DIM ** (-0.5)
    return jnp.where(allowed, scores, -1e30)


def allowed_of(length, slots):
    rows_at = lax.broadcasted_iota(jnp.int32, (slots, slots), 0)
    cols_at = lax.broadcasted_iota(jnp.int32, (slots, slots), 1)
    return (cols_at <= rows_at) & (cols_at < length)


def head_parts(packed, head, columns):
    return [
        packed[:, part * columns + head * HEAD_DIM : part * columns + (head + 1) * HEAD_DIM]
        for part in range(3)
    ]


def attention(pieces, gain, weight, lengths):
    count, (slots, features) = len(pieces), pieces[0].shape
    columns = weight.shape[1] // 3
    raw = gain is not None

    def kernel(lengths_ref, *refs):
        ins, weight_ref, refs = refs[:count], refs[count], refs[count + 1 :]
        if raw:
            gain_ref, refs = refs[0], refs[1:]
        packed_ref, level_ref, outs = refs[0], refs[1], refs[2 : count + 2]
        levels = []
        for j in range(count):
            if raw:
                rows = low(layer_norm(ins[j][...].astype(F32), gain_ref[...])[0])
                refs[count + 2 + j][...] = rows
            else:
                rows = ins[j][...]
            packed = low(product(rows, weight_ref[...], 1, 0))
            packed_ref[j] = packed
            allowed = allowed_of(lengths_ref[j], slots)
            found = []
            for head in range(columns // HEAD_DIM):
                queries, keys, values = head_parts(packed, head, columns)
                scores = masked_scores(queries, keys, allowed)
                top = jnp.max(scores, axis=-1, keepdims=True)
                raised = jnp.exp(scores - top)
                weight_sum = jnp.sum(raised, axis=-1, keepdims=True)
                levels.append(top + jnp.log(weight_sum))
                found.append(product(low(raised / weight_sum), values, 1, 0))
            outs[j][...] = low(jnp.concatenate(found, axis=1))
        level_ref[...] = jnp.concatenate(levels, axis=1)

    outs = [shape((count, slots, 3 * columns), LOW)]
    outs += [shape((slots, count * columns // HEAD_DIM), F32)]
    outs += [shape((slots, columns), LOW)] * count
    arrays = list(pieces) + [weight]
    if raw:
        outs += [shape((slots, features), LOW)] * count
        arrays.append(gain[None])
    flops = 2 * count * slots * features * 3 * columns
    packed, levels, *found = call(kernel, outs, [lengths], arrays, flops=flops)
    return (packed, levels), found[:count], found[count:] if raw else pieces


def attention_back(packed, grads, lengths):
    packed, levels = packed
    count, (slots, columns) = len(grads), grads[0].shape
    scaling = HEAD_DIM ** (-0.5)

    def kernel(lengths_ref, packed_ref, level_ref, *refs):
        out = refs[count]
        for j in range(count):
            allowed = allowed_of(lengths_ref[j], slots)
            whole = packed_ref[j]
            grad_whole = refs[j][...]
            found = [[], [], []]
            for head in range(columns // HEAD_DIM):
                queries, keys, values = head_parts(whole, head, columns)
                grad_head = grad_whole[:, head * HEAD_DIM : (head + 1) * HEAD_DIM]
                at = j * (columns // HEAD_DIM) + head
                scores = masked_scores(queries, keys, allowed)
                softened = jnp.exp(scores - level_ref[:, at : at + 1])
                grad_soft = product(grad_head, values, 1, 1)
                inner = jnp.sum(softened * grad_soft, axis=-1, keepdims=True)
                grad_scores = low(softened * (grad_soft - inner))
                found[0].append(scaling * product(grad_scores, keys, 1, 0))
                found[1].append(scaling * product(grad_scores, queries, 0, 0))
                found[2].append(product(low(softened), grad_head, 0, 0))
            out[j * slots : (j + 1) * slots, :] = low(
                jnp.concatenate(found[0] + found[1] + found[2], axis=1)
            )

    outs = [shape((count * slots, 3 * columns), LOW)]
    return call(kernel, outs, [lengths], [packed, levels] + list(grads))[0]


def normed_back(grad_packed, weight, count):
    slots, features = grad_packed.shape[0] // count, weight.shape[0]

    def kernel(grad_ref, weight_ref, *outs):
        whole = low(product(grad_ref[...], weight_ref[...], 1, 1))
        for j in range(count):
            outs[j][...] = whole[j * slots : (j + 1) * slots]

    outs = [shape((slots, features), LOW)] * count
    flops = 2 * count * slots * features * weight.shape[1]
    return call(kernel, outs, [], [grad_packed, weight], flops=flops)


def wide_across(own):
    return [own] + [swap(own, "wide", apart) for apart in range(2, lax.axis_size("wide"), 2)]


def wide_pieces(own):
    across = wide_across(own)
    return across, [swap(piece, "wide", 1) for piece in across]


def wide_join(pieces):
    across, beside = pieces
    return join_rows(list(across) + list(beside))


def wide_sends(own, received, slots):
    parts = pair_sum(own, received, slots)
    return [parts[0]] + [swap(p, "wide", 2 * (i + 1)) for i, p in enumerate(parts[1:])]


def wide_total(parts):
    total = parts[0]
    for part in parts[1:]:
        total = total + part.astype(F32)
    return total


def wide_sums(halves, slots):
    own, other = halves
    return wide_total(wide_sends(own, swap(other, "wide", 1), slots))


def place(labels, experts, capacity):
    blocks, slots = labels.shape
    first = jnp.arange(blocks, dtype=jnp.int32)[:, None] * capacity - 1
    places = jnp.arange(blocks * capacity, dtype=jnp.int32)
    selects = []
    for expert in experts:
        chosen = labels == expert
        at = jnp.where(chosen, first + jnp.cumsum(chosen.astype(jnp.int32), axis=1), -1)
        selects.append(low(places[:, None] == at.reshape(-1)[None, :]))
    return selects


def picked(selects, rows):
    return [low(product(select, rows, 1, 0)) for select in selects]


def exchanged(sent, slices):
    narrow = lax.axis_size("narrow")
    return join_rows(
        [sent[j // slices] if j == 0 else swap(sent[j // slices], "narrow", j) for j in range(narrow)]
    )


def to_experts(selects, rows, slices):
    return exchanged(picked(selects, rows), slices)


def from_experts(selects, outcome, slices):
    narrow = lax.axis_size("narrow")
    parts = outcome.reshape(narrow, -1, outcome.shape[-1])
    found = []
    for r in range(len(selects)):
        total = None
        for j in range(r * slices, (r + 1) * slices):
            part = parts[j] if j == 0 else swap(low(parts[j]), "narrow", j).astype(F32)
            total = part if total is None else total + part
        found.append(low(total))
    return found


def spread_of(selects, found, at):
    total = None
    for select, rows in zip(selects, found):
        part = product(select[:, at], rows, 0, 0)
        total = part if total is None else total + part
    return total


def layer_forward(source, raw, weights, selects, lengths, at_narrow, slices, second_work=None, third_work=None):
    norm_first, attention_in, attention_out, norm_second, mixer, up, down, expert_up, expert_down = weights
    slots, features = source.shape
    wide, narrow = lax.axis_size("wide"), lax.axis_size("narrow")
    normed, scaled_one, inverse_one = layer_norm(source, norm_first)
    own = low(normed)
    pieces = raw
    if raw is None:
        pieces = [own] + [swap(own, "narrow", j) for j in range(1, narrow)]
    packed, contexts, pieces = attention(
        pieces, None if raw is None else norm_first, attention_in, lengths
    )
    context, middle, second, scaled_two, inverse_two = attended(
        [contexts[0]] + [swap(contexts[j], "narrow", j) for j in range(1, narrow)],
        attention_out, source, norm_second, at_narrow,
    )
    across, beside = wide_pieces(second)
    if second_work is not None:
        across, second_found = together(across, second_work(second))
    rows = wide_join((across, beside))
    mixing = jax.nn.softmax(jnp.dot(rows, mixer, preferred_element_type=F32), axis=-1)
    pre = jnp.dot(rows, up, preferred_element_type=F32)
    act = low(activate(pre))
    third_found = None if third_work is None else third_work(rows, second_found)
    expert_rows, (mixing, pre, act, third_found) = together(
        to_experts(selects, rows, slices), (mixing, pre, act, third_found)
    )
    expert_pre = jnp.dot(expert_rows, expert_up, preferred_element_type=F32)
    expert_act = low(activate(expert_pre))
    kept = (
        scaled_one, inverse_one, pieces, packed, context, scaled_two, inverse_two,
        (rows, mixing, expert_rows, expert_pre, expert_act, pre, act),
    )
    return (middle, kept) if second_work is None else (middle, kept, third_found)


def experts_found(kept, weights, selects, slices, gate=None):
    act = kept[7][4] if gate is None else after(kept[7][4], gate)
    outcome = jnp.dot(act, weights[8], preferred_element_type=F32)
    return from_experts(selects, outcome, slices)


def merged_halves(kept, weights, selects, found, slots):
    mixing, act = kept[7][1], kept[7][6]

    def merged(at):
        dense = jnp.dot(act[at], weights[6], preferred_element_type=F32)
        return mixing[at, :1] * dense + mixing[at, 1:] * spread_of(selects, found, at)

    half = act.shape[0] // 2
    return merged(slice(0, half)), low(merged(slice(half, 2 * half)))


def dense_back_of(through, kept, weights):
    rows, mixing, _, _, _, pre, act = kept[7]
    dense_dot = jnp.sum(act.astype(F32) * through, axis=1, keepdims=True)
    dense_logit = mixing[:, :1] * mixing[:, 1:] * dense_dot
    grad_pre = low(activation_back(pre, mixing[:, :1] * through))
    return grad_pre, dense_logit


def experts_back(upstream, gathered, kept, weights, selects, slices, beneath, alongside):
    norm_second, mixer, up, down, expert_up, expert_down = weights[3:]
    scaled_two, inverse_two = kept[5:7]
    rows, mixing, expert_rows, expert_pre, expert_act, pre, act = kept[7]
    slots = upstream.shape[0]
    wide = lax.axis_size("wide")
    mixer_gap = (mixer[:, 0].astype(F32) - mixer[:, 1].astype(F32))[None]
    grads, expert_grads, through, dense_back = gathered
    expert_mixing = jax.nn.softmax(
        jnp.dot(expert_rows, mixer, preferred_element_type=F32), axis=-1
    )
    expert_dot = jnp.sum(expert_act.astype(F32) * through, axis=1, keepdims=True)
    expert_logit = -expert_mixing[:, :1] * expert_mixing[:, 1:] * expert_dot
    expert_grad_pre = low(activation_back(expert_pre, expert_mixing[:, 1:] * through))
    expert_back = product(expert_grad_pre, expert_up, 1, 1) + expert_logit * mixer_gap
    if callable(dense_back):
        dense_back = dense_back(expert_back)
    grad_pre, dense_logit = dense_back
    dense = (rows, grad_pre, act, mixing[:, :1], grads)
    found = from_experts(selects, expert_back, slices)
    experts = (
        expert_rows, expert_grad_pre,
        expert_act, expert_mixing[:, 1:], expert_grads,
    )
    found, beneath_found = together(found, beneath(expert_back, experts, dense))

    def merged(at):
        dense_back = product(grad_pre[at], up, 1, 1) + dense_logit[at] * mixer_gap
        return dense_back + spread_of(selects, found, at)

    half = grad_pre.shape[0] // 2
    halves = merged(slice(0, half)), low(merged(slice(half, 2 * half)))
    parts = wide_sends(halves[0], swap(halves[1], "wide", 1), slots)
    rows, dense_logit, expert_rows, expert_logit = after(
        (rows, dense_logit, expert_rows, expert_logit), parts[0]
    )
    grad_gap = jnp.sum(rows.astype(F32) * dense_logit, axis=0) + jnp.sum(
        expert_rows.astype(F32) * expert_logit, axis=0
    )
    grad_second, (grad_gap, alongside_found) = together(
        wide_total(parts), (grad_gap, alongside(parts[0], halves[1], beneath_found, experts, dense))
    )
    grad_norm_part, grad_norm_second = norm_back(grad_second, scaled_two, inverse_two, norm_second)
    return (
        upstream + grad_norm_part, dense, experts, (grad_norm_second, grad_gap),
        beneath_found, alongside_found,
    )


def up_product(parts):
    return product(parts[0], parts[1], 0, 0)


def down_product(parts):
    act, mix, grads = parts[2:]
    return product(act, low(mix * grads.astype(F32)), 0, 0)


def attention_grads(grad_middle, kept, weights, lengths, at_narrow, hold, filler):
    norm_first, attention_in, attention_out = weights[:3]
    scaled_one, inverse_one, pieces, packed, context = kept[:5]
    narrow = lax.axis_size("narrow")
    grad_attended = low(grad_middle)
    grad_contexts = context_back(grad_attended, attention_out, narrow, at_narrow)
    grad_contexts = [grad_contexts[0]] + [
        swap(grad_contexts[j], "narrow", j) for j in range(1, narrow)
    ]
    grad_packed = attention_back(packed, grad_contexts, lengths)
    grad_packed, hold = together(grad_packed, hold)
    parts = normed_back(grad_packed, attention_in, narrow)
    weight_grads = (pieces, after(grad_packed, parts), context, grad_attended)
    filled = filler(parts[0])
    parts = [parts[0]] + [swap(parts[j], "narrow", j) for j in range(1, narrow)]
    parts, filled = together(parts, filled)
    grad_normed = sum(part.astype(F32) for part in parts)
    grad_norm_part, grad_norm_first = norm_back(grad_normed, scaled_one, inverse_one, norm_first)
    return grad_middle + grad_norm_part, grad_norm_first, weight_grads, hold, filled


def last_grads(
    grad_middle, kept, weights, lengths, at_narrow, at_wide, dense, pair, narrow_columns, early
):
    norm_first, attention_in, attention_out = weights[:3]
    scaled_one, inverse_one, pieces, packed, context = kept[:5]
    narrow = lax.axis_size("narrow")
    grad_attended = low(grad_middle)
    grad_contexts = context_back(grad_attended, attention_out, narrow, at_narrow)
    grad_contexts = [grad_contexts[0]] + [
        swap(grad_contexts[j], "narrow", j) for j in range(1, narrow)
    ]
    out_halves = outer_halves([context], after(grad_attended, grad_contexts[-1]), at_wide)
    grad_contexts, out_halves = together(grad_contexts, halving_step(out_halves, 1))
    rows = pair.shape[0]
    gathered = narrow_gather(stack_own(dense, after(pair, grad_contexts), narrow_columns))
    out_halves = halving_step(out_halves, 2)
    early = after(early, grad_contexts)
    early = early + swap(early, "narrow", 1)
    grad_packed = attention_back(packed, grad_contexts, lengths)
    grad_packed, (out_halves, early) = together(grad_packed, (out_halves, early))
    in_halves = outer_halves(pieces, grad_packed, at_wide)
    in_halves, early = together(in_halves, axis_sum(early, "narrow", 2))
    parts = normed_back(after(grad_packed, in_halves), attention_in, narrow)
    in_halves = halving_step(halving_step(in_halves, 1), 2)
    parts = [parts[0]] + [swap(parts[j], "narrow", j) for j in range(1, narrow)]
    parts = after(parts, in_halves)
    grad_normed = sum(part.astype(F32) for part in parts)
    grad_norm_part, grad_norm_first = norm_back(grad_normed, scaled_one, inverse_one, norm_first)
    grad_inputs = grad_middle + grad_norm_part
    out_sum = halving_rest(out_halves, 4)
    in_sum, (first, grad_inputs) = together(
        low(halving_rest(in_halves, 4)), (grad_norm_first[None], grad_inputs)
    )
    out_sum = after(out_sum, in_halves)
    out_sum = out_sum + swap(low(out_sum), "narrow", 1).astype(F32)
    in_pieces = [in_sum] + [swap(in_sum, "narrow", j) for j in range(1, narrow)]
    in_pieces, gathered = together(
        in_pieces, split_gathered(after(gathered, in_sum), rows, narrow_columns)
    )
    vectors = axis_sum(jnp.concatenate([axis_sum(first, "narrow"), early], axis=0), "wide")
    spread = spread_columns(in_pieces, at_narrow)
    out_sum = after(out_sum, in_sum)
    distance = 2
    while distance < narrow:
        received = swap(low(out_sum), "narrow", distance)
        distance *= 2
        if distance >= narrow:
            received = after(received, spread)
        out_sum = out_sum + received.astype(F32)
    return grad_inputs, (spread, out_sum), vectors, gathered


def body(
    inputs, cotangent, seq_len, shallow_routes, deep_routes,
    shallow_norm_first, shallow_attention_in, shallow_attention_out, shallow_norm_second,
    shallow_dense_up, shallow_dense_down, shallow_mixer, shallow_expert_up, shallow_expert_down,
    deep_norm_first, deep_attention_in, deep_attention_out, deep_norm_second,
    deep_dense_up, deep_dense_down, deep_mixer, deep_expert_up, deep_expert_down,
):
    wide, narrow = lax.axis_size("wide"), lax.axis_size("narrow")
    wide_at, narrow_at = lax.axis_index("wide"), lax.axis_index("narrow")
    at_wide, at_narrow = wide_at.reshape(1), narrow_at.reshape(1)
    slots, features = inputs.shape
    small = jnp.stack(
        [
            shallow_norm_first, shallow_norm_second, deep_norm_first, deep_norm_second,
            shallow_mixer[:, 0], shallow_mixer[:, 1], deep_mixer[:, 0], deep_mixer[:, 1],
        ]
    )
    narrow_columns = 3 * features // narrow
    rows_own = shallow_attention_in.shape[0]
    input_pieces = [inputs] + [swap(inputs, "narrow", j) for j in range(1, narrow)]
    across = wide_across(own_slab(shallow_attention_in, None, at_narrow, small))
    lengths = seq_len[wide_at * narrow + (narrow_at ^ jnp.arange(narrow))]
    deep_slab = own_slab(deep_attention_in, None, at_narrow, None)
    across, (input_pieces, lengths, deep_slab) = together(
        across, (input_pieces, lengths, deep_slab)
    )
    in_pieces = across, [swap(piece, "wide", 1) for piece in across]
    shallow_in, small = join_slab(
        in_pieces, rows_own, [narrow_columns], at_wide, small.shape[0]
    )
    shallow_out = gather_wide(after(shallow_attention_out, across[1]))
    small = jnp.transpose(small.reshape(wide, 8, -1), (1, 0, 2)).reshape(8, features)
    gains = small[:4].astype(F32)
    def selects_of(routes, slices):
        table = routes.reshape(wide, narrow, slots)
        own = lax.dynamic_index_in_dim(table, narrow_at, axis=1, keepdims=False)
        capacity = slices * max(1, 3 * slots // (2 * wide * narrow))
        groups = narrow // slices
        experts = [wide_at * groups + ((narrow_at // slices) ^ r) for r in range(groups)]
        order = jnp.array(list(range(0, wide, 2)) + list(range(1, wide, 2)))
        return place(own[wide_at ^ order], experts, capacity)

    shallow_selects = selects_of(shallow_routes, SLICES_SHALLOW)
    deep_selects = selects_of(deep_routes, SLICES_DEEP)
    shallow = (
        gains[0], shallow_in, shallow_out, gains[1], small[4:6].T,
        shallow_dense_up, shallow_dense_down, shallow_expert_up[0], shallow_expert_down[0],
    )
    middle, kept_shallow = layer_forward(
        inputs.astype(F32), input_pieces, shallow, shallow_selects, lengths, at_narrow, SLICES_SHALLOW
    )
    deep_in = gather_wide(after(deep_slab, kept_shallow[7][0]))
    deep_out = gather_wide(after(deep_attention_out, kept_shallow[7][2]))
    found = experts_found(kept_shallow, shallow, shallow_selects, SLICES_SHALLOW)
    halves = merged_halves(kept_shallow, shallow, shallow_selects, found, slots)
    total = wide_sums(halves, slots)
    passed = middle + total
    all_grads = gather_wide(after(cotangent, total))
    deep = (
        gains[2], deep_in, deep_out, gains[3], small[6:8].T,
        deep_dense_up, deep_dense_down, deep_expert_up[0], deep_expert_down[0],
    )
    def second_work(second):
        grads = reorder(after(all_grads, second), slots, at_wide, False)
        expert_grads = to_experts(deep_selects, grads, SLICES_DEEP)
        return grads, expert_grads, product(grads, deep_dense_down, 1, 1)

    def third_work(rows, found):
        grads, expert_grads, through = found
        return grads, expert_grads, through, product(after(expert_grads, rows), deep_expert_down[0], 1, 1)

    middle, kept_deep, gathered = layer_forward(
        passed, None, deep, deep_selects, lengths, at_narrow, SLICES_DEEP, second_work, third_work
    )
    def deep_result(found):
        halves = merged_halves(kept_deep, deep, deep_selects, found, slots)
        return reorder(
            jnp.concatenate([low(halves[0]), halves[1]], axis=0), slots, at_wide, True
        )

    grad_middle, _, deep_experts, deep_rows, (whole, found), result = experts_back(
        cotangent.astype(F32),
        gathered[:2] + (
            gathered[3],
            lambda token: dense_back_of(after(gathered[2], token), kept_deep, deep),
        ), kept_deep,
        deep, deep_selects, SLICES_DEEP,
        lambda token, experts, dense: (
            dense_join(dense_products(after(dense, token))),
            experts_found(kept_deep, deep, deep_selects, SLICES_DEEP, token),
        ),
        lambda token, other, found, experts, dense: deep_result(after(found[1], token)),
    )
    total = lax.psum_scatter(result, "wide", scatter_dimension=0, tiled=True)
    grad_passed, deep_first, outer_parts, whole, deep_down = attention_grads(
        grad_middle, kept_deep, deep, lengths, at_narrow, narrow_scatter(whole),
        lambda token: down_product(after(deep_experts, token)),
    )
    passed_low = low(grad_passed)
    across, beside = wide_pieces(passed_low)
    across, total = together(across, total)
    grads = wide_join((across, beside))
    pair = outer_pair(*after(outer_parts, grads))
    expert_grads, (pair, dense_back) = together(
        to_experts(shallow_selects, grads, SLICES_SHALLOW),
        (
            pair,
            dense_back_of(product(grads, shallow_dense_down, 1, 1), kept_shallow, shallow),
        ),
    )
    pair = lax.psum_scatter(pair, "wide", scatter_dimension=0, tiled=True)
    whole = narrow_gather(after(whole, passed_low))
    grad_middle, _, _, shallow_rows, (joined, deep_up), (shallow_experts, pair, deep_dense) = experts_back(
        grad_passed,
        (grads, expert_grads, product(expert_grads, shallow_expert_down[0], 1, 1), dense_back),
        kept_shallow, shallow, shallow_selects, SLICES_SHALLOW,
        lambda token, experts, dense: (
            dense_join(dense_products(after(dense, token))),
            up_product(after(deep_experts, token)),
        ),
        lambda token, other, found, experts, dense: (
            [f(after(experts, token)) for f in (up_product, down_product)], pair,
            dense_outputs(after(whole, token)),
        ),
    )
    shallow_up, shallow_down = shallow_experts
    early = jnp.stack(list(shallow_rows) + [deep_first] + list(deep_rows))
    grad_inputs, (grad_shallow_in, grad_shallow_out), vectors, gathered = last_grads(
        grad_middle, kept_shallow, shallow, lengths, at_narrow, at_wide,
        narrow_scatter(joined), pair, narrow_columns, early,
    )
    *shallow_dense, grad_deep_in, grad_deep_out = gathered
    output = middle + total.astype(F32)
    deep_up, deep_down = deep_up[None], deep_down[None]
    shallow_up, shallow_down = shallow_up[None], shallow_down[None]
    grads_shallow = (
        grad_shallow_in, grad_shallow_out, *shallow_dense, shallow_up, shallow_down,
    )
    grads_deep = (
        grad_deep_in, grad_deep_out, *deep_dense, deep_up, deep_down,
    )
    vectors = lax.dynamic_slice_in_dim(vectors, wide_at * (features // wide), features // wide, axis=1)

    def outputs_of(grads, rows):
        grad_mixer = jnp.stack([rows[2], -rows[2]], axis=1)
        return (
            rows[0], grads[0], grads[1], rows[1], grads[2], grads[3], grad_mixer, grads[4], grads[5],
        )

    return (
        (low(output), grad_inputs)
        + outputs_of(grads_shallow, vectors[:3])
        + outputs_of(grads_deep, vectors[3:])
    )


def solution(mesh):
    both = ("wide", "narrow")
    parameters = (
        P("wide"), P("wide", None), P("wide", None), P("wide"), P(None, "wide"),
        P("wide", None), P("wide", None), P(both, None, None), P(both, None, None),
    )
    return jax.shard_map(
        body,
        mesh=mesh,
        in_specs=(P(both, None), P(both, None), P(), P(), P()) + parameters + parameters,
        out_specs=(P(both, None), P(both, None)) + parameters + parameters,
        check_vma=False,
    )
```
